32 devices in a mesh: groups: 2 (over x), dp: 8 (over z, y), expert: 2 (over core).
Axes of the slice: x: 2, y: 2, z: 4, core: 2. Of those that a mesh axis runs over, the one named last changes fastest.
Arguments:
- tokens: bfloat16 [128, 4096], P(('groups', 'dp', 'expert')), parts along dimension 0, may hold values from -6 to 6
- cotangent: bfloat16 [128, 4096], P(('groups', 'dp', 'expert')), parts along dimension 0, may hold values from -6 to 6
- routing: int32 [128, 2], P(('groups', 'dp', 'expert')), parts along dimension 0, may hold values from 0 to 7, as said below
- gate_first: int32 [128], P(('groups', 'dp', 'expert')), parts along dimension 0, may hold values from 1 to 1023
- gate_weight: bfloat16 [4096, 65536], P(None, ('dp', 'expert')), may hold values from -0.09375 to 0.09375
- up_weight: bfloat16 [4096, 65536], P(None, ('dp', 'expert')), may hold values from -0.09375 to 0.09375
- down_weight: bfloat16 [65536, 4096], P(('dp', 'expert')), may hold values from -0.0625 to 0.0625
Outputs:
- mixed: bfloat16 [128, 4096], P(('groups', 'dp', 'expert')), parts along dimension 0
- token_grad: bfloat16 [128, 4096], P(('groups', 'dp', 'expert')), parts along dimension 0
- gate_grad: float32 [128, 2], P(('groups', 'dp', 'expert')), parts along dimension 0
The draws below stay inside these ranges and needn't reach their ends.
There are 2 independent parts, one for each index of `groups`. The reference program is written for one: setup_inputs(seed, part) draws one part's arguments, and reference() takes and returns one part's arrays. A program takes and returns all parts, laid end to end along the dimension named above; an argument that names none is the same for every part. Nothing has to cross between parts.
Inputs may be any that keep to these rules, and one draw needn't show every extreme that they name: `routing`: the two experts of a token differ. Among the 4 tokens of one device (aligned blocks of 4 rows) no expert is named more than 2 times, and one expert is named exactly 2 times in every such block.
All inputs are finite; a program needn't handle non-finite values.
Results may differ from the reference program's by a relative error of at most 0.014.
Values may be sent and summed in bfloat16 or wider, within the bound.
A program may use at most 192 MiB of HBM per device.

```python
import jax
import jax.numpy as jnp
from jax import lax

D = 4096
E = 8
FF_WIN = 8192
TOK_DEV = 4
CAP = 2
TOKENS = 64
N_DP = 8
N_EXPERT = 2


def permute_rows(block_keys, length):

    def permute_one(one_key):
        return jax.random.permutation(one_key, length)
    return jax.vmap(permute_one)(block_keys)


def draw_routing(key, part):
    key_hot, key_order, key_shift, key_rows, key_swap = jax.random.split(key, 5)
    block_count = TOKENS // TOK_DEV
    hot_expert = jax.random.randint(key_hot, (), 0, E)
    others = permute_rows(jax.random.split(key_order, block_count), E - 1).astype(jnp.int32)
    others = (hot_expert + 1 + others) % E
    shift = jax.random.randint(key_shift, (block_count, 1), 0, CAP)
    positions = jnp.arange(2 * TOK_DEV, dtype=jnp.int32)[None, :]
    run_index = jnp.clip((positions - CAP + shift) // CAP, 0, E - 2)
    run_index = jnp.broadcast_to(run_index, (block_count, 2 * TOK_DEV))
    other_pick = jnp.take_along_axis(others, run_index, axis=1)
    listed = jnp.where(positions < CAP, hot_expert, other_pick)
    first_col = listed[:, :TOK_DEV]
    second_col = listed[:, TOK_DEV:]
    swap_bits = jax.random.randint(key_swap, (block_count, TOK_DEV), 0, 2)
    col_left = jnp.where(swap_bits == 1, second_col, first_col)
    col_right = jnp.where(swap_bits == 1, first_col, second_col)
    row_order = permute_rows(jax.random.split(key_rows, block_count), TOK_DEV).astype(jnp.int32)
    inverse = jnp.argsort(row_order, axis=1)
    col_left = jnp.take_along_axis(col_left, inverse, axis=1)
    col_right = jnp.take_along_axis(col_right, inverse, axis=1)
    return jnp.stack([col_left, col_right], axis=-1).reshape(TOKENS, 2).astype(jnp.int32)


def set_ends(result, own_key, low, top_value):
    shape = result.shape
    place = [jax.random.randint(jax.random.fold_in(own_key, axis), (), 0, shape[axis]) for axis in range(len(shape))]
    result = result.at[tuple(place)].set(low)
    longest = shape.index(max(shape))
    place[longest] = (place[longest] + 1) % shape[longest]
    return result.at[tuple(place)].set(top_value)


def level_of(rng, dims, pieces, least, high):
    loudness, own = 1.0, jax.random.fold_in(rng, 6)
    for dim, shards_of in pieces:
        heights = jnp.exp(jax.random.uniform(jax.random.fold_in(own, dim), (shards_of,), jnp.float32, least / len(pieces), high / len(pieces)))
        loudness = loudness * jnp.repeat(heights, dims[dim] // shards_of).reshape([-1 if axis == dim else 1 for axis in range(len(dims))])
    return loudness


def gaussian(stream_key, shape, deviation, limit, cuts=(), held_as=jnp.bfloat16):
    values = deviation * jax.random.normal(stream_key, shape, jnp.float32)
    if cuts:
        values = values * level_of(stream_key, shape, cuts, -0.22, 0.18)
    return jnp.clip(values, -limit, limit).astype(held_as)


def setup_inputs(seed: int = 0, part: int = 0) -> dict:
    arg_keys = jax.random.split(jax.random.key(seed), 8)
    part_keys = jax.random.split(jax.random.fold_in(arg_keys[7], part), 8)
    return {
        "tokens": gaussian(part_keys[0], (TOKENS, D), 1.0, 6.0, ((0, 16),)),
        "cotangent": gaussian(part_keys[1], (TOKENS, D), 1.0, 6.0, ((0, 16),)),
        "routing": draw_routing(jax.random.fold_in(jax.random.fold_in(arg_keys[7], part), 71), part),
        "gate_first": set_ends(jax.random.randint(part_keys[3], (TOKENS,), 1, 1024), jax.random.fold_in(part_keys[3], 1), 1, 1023).astype(jnp.int32),
        "gate_weight": gaussian(arg_keys[4], (D, E * FF_WIN), D ** -0.5, 0.09375, ((1, 16),)),
        "up_weight": gaussian(arg_keys[5], (D, E * FF_WIN), D ** -0.5, 0.09375, ((1, 16),)),
        "down_weight": gaussian(arg_keys[6], (E * FF_WIN, D), FF_WIN ** -0.5, 0.0625, ((0, 16),)),
    }


def block_sum(left, right_blocks):
    group_count = right_blocks.shape[0]
    block_width = right_blocks.shape[1]
    rows_here = left.shape[0]
    split_left = left.reshape(rows_here, group_count, block_width).astype(jnp.float32)
    terms = jnp.einsum("rgh,ghd->grd", split_left, right_blocks.astype(jnp.float32))
    return terms


def round_sum(terms):
    rounded = lax.optimization_barrier(terms.astype(jnp.bfloat16))
    return jnp.sum(rounded.astype(jnp.float32), axis=0)


def reference(tokens, cotangent, routing, gate_first, gate_weight, up_weight, down_weight):
    share_first = gate_first.astype(jnp.float32) / 1024.0
    share_second = (1024 - gate_first).astype(jnp.float32) / 1024.0
    most_rows = (TOKENS // TOK_DEV) * CAP
    group_count = (N_DP * N_EXPERT) // E
    block_width = FF_WIN // group_count

    def one_expert(carry, expert_id):
        mixed_sum, grad_sum, score_sum = carry
        in_first = routing[:, 0] == expert_id
        in_second = routing[:, 1] == expert_id
        chosen = in_first | in_second
        weight_all = jnp.where(in_first, share_first, 0.0) + jnp.where(in_second, share_second, 0.0)
        row_ids = jnp.nonzero(chosen, size=most_rows, fill_value=0)[0].astype(jnp.int32)
        live_rows = jnp.arange(most_rows, dtype=jnp.int32) < jnp.sum(chosen.astype(jnp.int32))
        row_weight = jnp.where(live_rows, weight_all[row_ids], 0.0)
        inputs = tokens[row_ids]
        grads_in = cotangent[row_ids]
        start = (expert_id * FF_WIN).astype(jnp.int32)
        w_gate = lax.dynamic_slice_in_dim(gate_weight, start, FF_WIN, 1)
        w_up = lax.dynamic_slice_in_dim(up_weight, start, FF_WIN, 1)
        w_down = lax.dynamic_slice_in_dim(down_weight, start, FF_WIN, 0)
        gate_pre = jnp.dot(inputs, w_gate, preferred_element_type=jnp.float32)
        up_pre = jnp.dot(inputs, w_up, preferred_element_type=jnp.float32)
        hidden = (jax.nn.silu(gate_pre) * up_pre).astype(jnp.bfloat16)
        expert_out = round_sum(block_sum(hidden, w_down.reshape(group_count, block_width, D)))
        score = jnp.sum(grads_in.astype(jnp.float32) * expert_out, axis=1)
        score = jnp.where(live_rows, score, 0.0)
        d_hidden = row_weight[:, None] * jnp.dot(grads_in, w_down.T, preferred_element_type=jnp.float32)
        sig_gate = jax.nn.sigmoid(gate_pre)
        d_gate = (d_hidden * up_pre * sig_gate * (1.0 + gate_pre * (1.0 - sig_gate))).astype(jnp.bfloat16)
        d_up = (d_hidden * jax.nn.silu(gate_pre)).astype(jnp.bfloat16)
        grad_terms = block_sum(d_gate, w_gate.T.reshape(group_count, block_width, D))
        grad_terms = grad_terms + block_sum(d_up, w_up.T.reshape(group_count, block_width, D))
        grad_rows = round_sum(grad_terms)
        mixed_sum = mixed_sum.at[row_ids].add(row_weight[:, None] * expert_out)
        grad_sum = grad_sum.at[row_ids].add(jnp.where(live_rows[:, None], grad_rows, 0.0))
        score_full = jnp.zeros((TOKENS,), jnp.float32).at[row_ids].add(score)
        score_sum = score_sum + jnp.stack([jnp.where(in_first, score_full, 0.0), jnp.where(in_second, score_full, 0.0)], axis=1)
        return (mixed_sum, grad_sum, score_sum), None

    start_carry = (jnp.zeros((TOKENS, D), jnp.float32), jnp.zeros((TOKENS, D), jnp.float32), jnp.zeros((TOKENS, 2), jnp.float32))
    final, _ = lax.scan(one_expert, start_carry, jnp.arange(E, dtype=jnp.int32))
    mixed_sum, grad_sum, score_sum = final
    return mixed_sum.astype(jnp.bfloat16), grad_sum.astype(jnp.bfloat16), score_sum
```

```python
import functools

import jax
import jax.numpy as jnp
from jax import lax
from jax.experimental import pallas as pl
from jax.experimental.pallas import tpu as pltpu
from jax.sharding import PartitionSpec as P

E = 8
X_CUTS = (2048, 2048)
OUT_CUTS = (4096,)
GRAD_CUTS = (1024, 1024, 1024, 1024)
ROWS_IN = 512
TILE = 16
NN = (((1,), (0,)), ((), ()))
NT = (((1,), (1,)), ((), ()))


def expert_rows(got_x, got_dy, got_w, gate_weight, up_weight, down_weight):
    gate_pre = jnp.dot(got_x, gate_weight, preferred_element_type=jnp.float32)
    up_pre = jnp.dot(got_x, up_weight, preferred_element_type=jnp.float32)
    sig_gate = jax.nn.sigmoid(gate_pre)
    silu_gate = gate_pre * sig_gate
    hidden = (silu_gate * up_pre).astype(jnp.bfloat16)
    part_out = jnp.dot(hidden, down_weight, preferred_element_type=jnp.float32)
    d_hidden = got_w[:, None] * jnp.dot(got_dy, down_weight.T, preferred_element_type=jnp.float32)
    d_gate = (d_hidden * up_pre * sig_gate * (1.0 + gate_pre * (1.0 - sig_gate))).astype(
        jnp.bfloat16
    )
    d_up = (d_hidden * silu_gate).astype(jnp.bfloat16)
    part_grad = jnp.dot(d_gate, gate_weight.T, preferred_element_type=jnp.float32)
    part_grad = part_grad + jnp.dot(d_up, up_weight.T, preferred_element_type=jnp.float32)
    return (part_out.astype(jnp.bfloat16), part_grad.astype(jnp.bfloat16))


def on_device(tokens, cotangent, routing, gate_first, gate_weight, up_weight, down_weight):
    devices = lax.axis_size(("dp", "expert"))
    group_size = devices // E
    tok_rows = tokens.shape[0]
    width = tokens.shape[1]
    capacity = tok_rows // 2
    expert_ids = jnp.arange(E, dtype=jnp.int32)
    first_hot = (routing[:, 0:1] == expert_ids[None, :]).astype(jnp.int32)
    second_hot = (routing[:, 1:2] == expert_ids[None, :]).astype(jnp.int32)
    hot = first_hot + second_hot
    row_ids = jnp.arange(tok_rows, dtype=jnp.int32)
    not_later = (row_ids[:, None] >= row_ids[None, :]).astype(jnp.int32)
    rank_rows = jnp.sum(not_later[:, :, None] * hot[None, :, :], axis=1) - 1
    slot_ids = jnp.arange(capacity, dtype=jnp.int32)
    slot_hot = (rank_rows[:, :, None] == slot_ids[None, None, :]).astype(jnp.float32)
    pick_first = first_hot[:, :, None].astype(jnp.float32) * slot_hot
    pick_second = second_hot[:, :, None].astype(jnp.float32) * slot_hot
    picked = pick_first + pick_second
    share_first = gate_first.astype(jnp.float32) / 1024.0
    share_second = (1024 - gate_first).astype(jnp.float32) / 1024.0
    picked_low = picked.astype(jnp.bfloat16)
    send_x = jnp.einsum(
        "tec,td->ecd", picked_low, tokens, preferred_element_type=jnp.float32
    ).astype(jnp.bfloat16)
    send_dy = jnp.einsum(
        "tec,td->ecd", picked_low, cotangent, preferred_element_type=jnp.float32
    ).astype(jnp.bfloat16)
    weighted = pick_first * share_first[:, None, None] + pick_second * share_second[:, None, None]
    send_w = jnp.sum(weighted, axis=0)
    out_x = jnp.repeat(send_x, group_size, axis=0)
    out_dy = jnp.repeat(send_dy, group_size, axis=0)
    out_w = jnp.repeat(send_w, group_size, axis=0)

    def exchange(value):
        return lax.all_to_all(value, ("dp", "expert"), split_axis=0, concat_axis=0, tiled=True)

    recv_x, recv_dy = exchange(out_x), exchange(out_dy)
    recv_w = exchange(out_w.astype(jnp.bfloat16)).astype(out_w.dtype)
    got_x = recv_x.reshape(devices * capacity, width)
    got_dy = recv_dy.reshape(devices * capacity, width)
    got_w = recv_w.reshape(devices * capacity)
    part_out, part_grad = expert_rows(got_x, got_dy, got_w, gate_weight, up_weight, down_weight)
    back_out = exchange(part_out.reshape(devices, capacity, width))
    back_grad = exchange(part_grad.reshape(devices, capacity, width))
    summed_out = jnp.sum(
        back_out.astype(jnp.float32).reshape(E, group_size, capacity, width), axis=1
    )
    summed_grad = jnp.sum(
        back_grad.astype(jnp.float32).reshape(E, group_size, capacity, width), axis=1
    )
    rank_first = jnp.take_along_axis(rank_rows, routing[:, 0:1], axis=1)[:, 0]
    rank_second = jnp.take_along_axis(rank_rows, routing[:, 1:2], axis=1)[:, 0]
    slot_first = routing[:, 0] * capacity + rank_first
    slot_second = routing[:, 1] * capacity + rank_second
    flat_out = summed_out.reshape(E * capacity, width)
    flat_grad = summed_grad.reshape(E * capacity, width)
    out_first = jnp.take(flat_out, slot_first, axis=0)
    out_second = jnp.take(flat_out, slot_second, axis=0)
    mixed = (share_first[:, None] * out_first + share_second[:, None] * out_second).astype(
        jnp.bfloat16
    )
    token_grad = (
        jnp.take(flat_grad, slot_first, axis=0) + jnp.take(flat_grad, slot_second, axis=0)
    ).astype(jnp.bfloat16)
    cot_float = cotangent.astype(jnp.float32)
    grad_first = jnp.sum(cot_float * out_first, axis=1)
    grad_second = jnp.sum(cot_float * out_second, axis=1)
    gate_grad = jnp.stack([grad_first, grad_second], axis=1)
    return (mixed, token_grad, gate_grad)


def spans(cuts, width):
    scale = width // sum(cuts)
    found, start = [], 0
    for cut in cuts:
        found.append((start, cut * scale))
        start += cut * scale
    return found


def one_hot(rows, columns, test):
    row = lax.broadcasted_iota(jnp.int32, (rows, columns), 0)
    col = lax.broadcasted_iota(jnp.int32, (rows, columns), 1)
    return jnp.where(test(row, col), 1.0, 0.0).astype(jnp.bfloat16)


def layer_kernel(
    n_dp,
    route_ref,
    first_ref,
    x_ref,
    dy_ref,
    gate_hbm,
    up_hbm,
    down_hbm,
    mixed_ref,
    grad_ref,
    score_ref,
    wide,
    down,
    both8,
    cot8,
    xs,
    dys,
    pre,
    hid,
    d_both,
    acc,
    pair_send,
    pair_recv,
    kept,
    side_send,
    side_recv,
    w_sem,
    in_sems,
    pass_sems,
    ring_sems,
    back_sems,
    packs,
    recvs,
    back_sends,
    back_recvs,
):
    tok, width = x_ref.shape
    cap = tok // 2
    segs = TILE // cap
    quarter = n_dp * cap
    rows = 4 * quarter
    lines = n_dp * TILE
    hidden = down_hbm.shape[0]
    part = hidden // 2
    grp = lax.axis_index("groups")
    dp = lax.axis_index("dp")
    core = lax.axis_index("expert")
    far, other = 1 - grp, 1 - core
    f32, bf16 = jnp.float32, jnp.bfloat16
    first_unit = pl.multiple_of(grp * part, part)

    def place(g, q, c):
        return {"groups": g, "dp": q, "expert": c}

    def remote(src, dst, send, arrive, where):
        return pltpu.make_async_remote_copy(
            src_ref=src,
            dst_ref=dst,
            send_sem=send,
            recv_sem=arrive,
            device_id=where,
            device_id_type=pl.DeviceIdType.MESH,
        )

    barrier = pltpu.get_barrier_semaphore()
    for where in [place(grp, lax.rem(dp + k, n_dp), core) for k in range(1, n_dp)] + [
        place(grp, dp, other),
        place(far, dp, core),
    ]:
        pl.semaphore_signal(
            barrier, inc=1, device_id=where, device_id_type=pl.DeviceIdType.MESH
        )

    wide_loads, down_loads = [], []
    for n in range(width // ROWS_IN):
        at = pl.ds(n * ROWS_IN, ROWS_IN)
        for m, ref in ((0, gate_hbm), (1, up_hbm)):
            wide_loads.append(
                pltpu.make_async_copy(
                    ref.at[at, pl.ds(first_unit, part)],
                    wide.at[at, pl.ds(m * part, part)],
                    w_sem.at[2 * n + m],
                )
            )
    for n in range(part // ROWS_IN):
        down_loads.append(
            pltpu.make_async_copy(
                down_hbm.at[pl.ds(first_unit + n * ROWS_IN, ROWS_IN), :],
                down.at[pl.ds(n * ROWS_IN, ROWS_IN), :],
                w_sem.at[2 * (width // ROWS_IN) + n],
            )
        )
    for copy in wide_loads + down_loads:
        copy.start()

    slots = []
    for t in range(tok):
        row = []
        for j in range(2):
            e = route_ref[j, t]
            rank = jnp.int32(0)
            for s in range(t):
                rank = rank + jnp.where((route_ref[0, s] == e) | (route_ref[1, s] == e), 1, 0)
            row.append(e * cap + rank)
        slots.append(row)

    x32, dy32 = x_ref[...].astype(f32), dy_ref[...].astype(f32)
    both8[0:tok, :] = x32
    both8[tok : 2 * tok, :] = dy32
    cot8[0:tok, :] = dy32
    cot8[tok : 2 * tok, :] = dy32

    def chosen_rows(offset):
        def test(row, col):
            hit = None
            for t in range(tok):
                mine = (row // segs == slots[t][0]) | (row // segs == slots[t][1])
                mine = mine & (col % (2 * tok) == offset + t)
                hit = mine if hit is None else hit | mine
            return hit & (row % segs == col // (2 * tok))

        return one_hot(lines, segs * 2 * tok, test)

    batches = [(0, start, size) for start, size in spans(X_CUTS, width)] + [(1, 0, width)]
    pick_rows = (chosen_rows(0), chosen_rows(tok))
    sends = []

    def pack(n):
        which, start, size = batches[n]
        step = size // segs
        stacked = jnp.concatenate(
            [both8[:, start + s * step : start + (s + 1) * step] for s in range(segs)], axis=0
        ).astype(bf16)
        lined = lax.dot_general(pick_rows[which], stacked, NN, preferred_element_type=f32)
        packs[n][...] = lined.astype(bf16).reshape(n_dp, TILE, step)

    def send(n):
        for k in range(1, n_dp):
            q = lax.rem(dp + k, n_dp)
            copy = remote(
                packs[n].at[q],
                recvs[n].at[grp, core, dp],
                in_sems.at[0, n, k],
                in_sems.at[1, n, k],
                place(grp, q, core),
            )
            copy.start()
            sends.append(copy)
        recvs[n][grp, core, dp] = packs[n][dp]

    pack(0)
    pl.semaphore_wait(barrier, n_dp + 1)
    send(0)
    for n in range(1, len(batches)):
        pack(n)
        send(n)

    to_pair, to_far, pair_on = {}, {}, {}

    def pass_on(n):
        for k in range(1, n_dp):
            sends[n * (n_dp - 1) + k - 1].wait_recv()
        mine = recvs[n].at[grp, core]
        to_far[n] = remote(
            mine, mine, pass_sems.at[0, n], pass_sems.at[1, n], place(far, dp, core)
        )
        to_pair[n] = remote(
            mine, mine, pass_sems.at[2, n], pass_sems.at[3, n], place(grp, dp, other)
        )
        to_far[n].start()
        to_pair[n].start()

    def pass_far(n):
        to_far[n].wait_recv()
        theirs = recvs[n].at[far, core]
        pair_on[n] = remote(
            theirs, theirs, pass_sems.at[4, n], pass_sems.at[5, n], place(grp, dp, other)
        )
        pair_on[n].start()

    unmix = one_hot(
        lines, lines, lambda row, col: (row // quarter == col % segs) & (row % quarter == col // segs)
    )
    mix = one_hot(
        lines, lines, lambda row, col: (col // quarter == row % segs) & (col % quarter == row // segs)
    )

    def unpack(n, dest):
        which, start, size = batches[n]
        step = size // segs
        to_pair[n].wait_recv()
        pair_on[n].wait_recv()
        for g in range(2):
            for c in range(2):
                lined = recvs[n][g, c].reshape(lines, step)
                flat = lax.dot_general(unmix, lined, NN, preferred_element_type=f32).astype(bf16)
                top = (2 * g + c) * quarter
                for s in range(segs):
                    dest[top : top + quarter, start + s * step : start + (s + 1) * step] = flat[
                        s * quarter : (s + 1) * quarter, :
                    ]

    def multiply_in(n, between):
        _, start, size = batches[n]
        for m in range(start // ROWS_IN, (start + size) // ROWS_IN):
            wide_loads[2 * m].wait()
            wide_loads[2 * m + 1].wait()
        block = 2 * part // 4
        for m in range(4):
            cols = slice(m * block, (m + 1) * block)
            term = lax.dot_general(
                xs[:, start : start + size],
                wide[start : start + size, cols],
                NN,
                preferred_element_type=f32,
            )
            pre[:, cols] = term if n == 0 else pre[:, cols] + term
            if m == 1:
                between()

    def first_between():
        pass_far(1)
        pass_on(2)

    pass_on(0)
    pass_on(1)
    pass_far(0)
    unpack(0, xs)
    multiply_in(0, first_between)
    unpack(1, xs)
    multiply_in(1, lambda: pass_far(2))
    unpack(2, dys)
    for copy in down_loads:
        copy.wait()

    block = part // 4
    for m in range(4):
        cols = slice(m * block, (m + 1) * block)
        more = slice(part + m * block, part + (m + 1) * block)
        d_hidden = lax.dot_general(down[cols, :], dys[...], NT, preferred_element_type=f32).T
        gate_pre, up_pre = pre[:, cols], pre[:, more]
        sig = 1.0 / (1.0 + jnp.exp(-gate_pre))
        silu = gate_pre * sig
        hid[:, cols] = (silu * up_pre).astype(bf16)
        d_both[:, cols] = (d_hidden * up_pre * sig * (1.0 + gate_pre * (1.0 - sig))).astype(bf16)
        d_both[:, more] = (d_hidden * silu).astype(bf16)

    items = [(0, start, size) for start, size in spans(OUT_CUTS, width)]
    items += [(1, start, size) for start, size in spans(GRAD_CUTS, width)]
    pair_copies, side_copies, home_copies = {}, {}, {}

    def compute(i):
        which, start, size = items[i]
        cols = slice(start, start + size)
        if which == 0:
            block = min(size, 1024)
            for at in range(start, start + size, block):
                acc[0, :, at : at + block] = lax.dot_general(
                    hid[...], down[:, at : at + block], NN, preferred_element_type=f32
                )
        else:
            acc[1, :, cols] = lax.dot_general(
                wide[cols, :], d_both[...], NT, preferred_element_type=f32
            ).T
        for g in range(2):
            give = pl.ds(pl.multiple_of((2 * g + other) * quarter, quarter), quarter)
            pair_send[which, g, :, cols] = acc[which, give, cols].astype(bf16)
        pair_copies[i] = remote(
            pair_send.at[which, :, :, pl.ds(start, size)],
            pair_recv.at[which, :, :, pl.ds(start, size)],
            ring_sems.at[0, i],
            ring_sems.at[1, i],
            place(grp, dp, other),
        )
        pair_copies[i].start()

    def to_side(i):
        which, start, size = items[i]
        cols = slice(start, start + size)
        pair_copies[i].wait_recv()

        def total(g):
            own = pl.ds(pl.multiple_of((2 * g + core) * quarter, quarter), quarter)
            return acc[which, own, cols] + pair_recv[which, g, :, cols].astype(f32)

        side_send[which, :, cols] = total(far).astype(bf16)
        side_copies[i] = remote(
            side_send.at[which, :, pl.ds(start, size)],
            side_recv.at[which, :, pl.ds(start, size)],
            ring_sems.at[2, i],
            ring_sems.at[3, i],
            place(far, dp, core),
        )
        side_copies[i].start()
        kept[which, :, cols] = total(grp)

    def to_home(i):
        which, start, size = items[i]
        step = size // segs
        side_copies[i].wait_recv()
        cols = slice(start, start + size)
        total = (kept[which, :, cols] + side_recv[which, :, cols].astype(f32)).astype(bf16)
        stacked = jnp.concatenate([total[:, s * step : (s + 1) * step] for s in range(segs)], axis=0)
        lined = lax.dot_general(mix, stacked, NN, preferred_element_type=f32).astype(bf16)
        back_sends[i][...] = lined.reshape(n_dp, TILE, step)
        home_copies[i] = []
        for k in range(1, n_dp):
            q = lax.rem(dp + k, n_dp)
            copy = remote(
                back_sends[i].at[q],
                back_recvs[i].at[dp],
                back_sems.at[0, i, k],
                back_sems.at[1, i, k],
                place(grp, q, core),
            )
            copy.start()
            home_copies[i].append(copy)
        back_recvs[i][dp] = back_sends[i][dp]

    def pick_test(row, col):
        hit = None
        for t in range(tok):
            for j in range(2):
                mine = (row % (2 * tok) == j * tok + t) & (col // segs == slots[t][j])
                hit = mine if hit is None else hit | mine
        return hit & (row // (2 * tok) == col % segs)

    pick = one_hot(segs * 2 * tok, lines, pick_test)
    share_rows = lax.broadcasted_iota(jnp.int32, (2 * tok, 1), 0)
    units = jnp.zeros((2 * tok, 1), jnp.int32)
    for t in range(tok):
        units = jnp.where(share_rows == t, first_ref[t], units)
        units = jnp.where(share_rows == tok + t, 1024 - first_ref[t], units)
    share = units.astype(f32) / 1024.0
    scores = []

    def finish(i):
        which, start, size = items[i]
        step = size // segs
        for copy in home_copies[i]:
            copy.wait_recv()
        got = lax.dot_general(
            pick, back_recvs[i][...].reshape(lines, step), NN, preferred_element_type=f32
        )
        for s in range(segs):
            cols = slice(start + s * step, start + (s + 1) * step)
            here = got[s * 2 * tok : (s + 1) * 2 * tok, :]
            weighted = here * share
            summed = (weighted[:tok] + weighted[tok:]).astype(bf16)
            if which == 0:
                mixed_ref[:, cols] = summed
                scores.append(jnp.sum(here * cot8[:, cols], axis=1, keepdims=True))
            else:
                grad_ref[:, cols] = summed

    compute(0)
    compute(1)
    to_side(0)
    compute(2)
    to_side(1)
    compute(3)
    to_home(0)
    to_side(2)
    to_home(1)
    compute(4)
    to_side(3)
    to_home(2)

    to_side(4)
    to_home(3)
    finish(0)

    finish(1)
    to_home(4)
    finish(2)

    for i in range(3, len(items)):
        finish(i)

    score = scores[0]
    for more in scores[1:]:
        score = score + more
    row = lax.broadcasted_iota(jnp.int32, (2 * tok, tok), 0)
    col = lax.broadcasted_iota(jnp.int32, (2 * tok, tok), 1)
    for j in range(2):
        score_ref[j : j + 1, :] = jnp.sum(
            jnp.where(row == col + j * tok, score, 0.0), axis=0, keepdims=True
        )

    for copy in sends:
        copy.wait_send()
    for copies in (to_far, to_pair, pair_on, pair_copies, side_copies):
        for copy in copies.values():
            copy.wait_send()
    for copies in home_copies.values():
        for copy in copies:
            copy.wait_send()


def place_kernel(mixed_in, grad_in, score_in, mixed_out, grad_out, score_out):
    mixed_out[...] = mixed_in[...]
    grad_out[...] = grad_in[...]
    score_out[...] = score_in[...]


def fused(n_dp, tokens, cotangent, routing, gate_first, gate_weight, up_weight, down_weight):
    tok, width = tokens.shape
    cap = tok // 2
    segs = TILE // cap
    quarter = n_dp * cap
    rows = 4 * quarter
    hidden = down_weight.shape[0]
    part = hidden // 2
    f32, bf16 = jnp.float32, jnp.bfloat16
    vmem = pl.BlockSpec(memory_space=pltpu.VMEM)
    smem = pl.BlockSpec(memory_space=pltpu.SMEM)
    hbm = pl.BlockSpec(memory_space=pl.ANY)
    dma = pltpu.SemaphoreType.DMA
    steps_in = [size // segs for _, size in spans(X_CUTS, width)] + [width // segs]
    steps_out = [size // segs for _, size in spans(OUT_CUTS, width) + spans(GRAD_CUTS, width)]
    shapes = (
        jax.ShapeDtypeStruct((tok, width), bf16),
        jax.ShapeDtypeStruct((tok, width), bf16),
        jax.ShapeDtypeStruct((2, tok), f32),
    )
    results = pl.pallas_call(
        functools.partial(layer_kernel, n_dp),
        out_shape=shapes,
        in_specs=[smem, smem, vmem, vmem, hbm, hbm, hbm],
        out_specs=(vmem, vmem, vmem),
        scratch_shapes=[
            pltpu.VMEM((width, 2 * part), bf16),
            pltpu.VMEM((part, width), bf16),
            pltpu.VMEM((2 * tok, width), f32),
            pltpu.VMEM((2 * tok, width), f32),
            pltpu.VMEM((rows, width), bf16),
            pltpu.VMEM((rows, width), bf16),
            pltpu.VMEM((rows, 2 * part), f32),
            pltpu.VMEM((rows, part), bf16),
            pltpu.VMEM((rows, 2 * part), bf16),
            pltpu.VMEM((2, rows, width), f32),
            pltpu.VMEM((2, 2, quarter, width), bf16),
            pltpu.VMEM((2, 2, quarter, width), bf16),
            pltpu.VMEM((2, quarter, width), f32),
            pltpu.VMEM((2, quarter, width), bf16),
            pltpu.VMEM((2, quarter, width), bf16),
            dma((2 * (width // ROWS_IN) + part // ROWS_IN,)),
            dma((2, len(steps_in), n_dp)),
            dma((6, len(steps_in))),
            dma((4, len(steps_out))),
            dma((2, len(steps_out), n_dp)),
            [pltpu.VMEM((n_dp, TILE, step), bf16) for step in steps_in],
            [pltpu.VMEM((2, 2, n_dp, TILE, step), bf16) for step in steps_in],
            [pltpu.VMEM((n_dp, TILE, step), bf16) for step in steps_out],
            [pltpu.VMEM((n_dp, TILE, step), bf16) for step in steps_out],
        ],
        compiler_params=pltpu.CompilerParams(
            collective_id=0, has_side_effects=True, vmem_limit_bytes=61 * 1024 * 1024
        ),
    )(routing.T, gate_first, tokens, cotangent, gate_weight, up_weight, down_weight)
    mixed, grad, score = pl.pallas_call(
        place_kernel,
        out_shape=shapes,
        in_specs=[vmem] * 3,
        out_specs=(vmem, vmem, vmem),
    )(*results)
    return mixed, grad, score.T


def solution(mesh):
    placed = (
        P(("groups", "dp", "expert"), None),
        P(("groups", "dp", "expert"), None),
        P(("groups", "dp", "expert"), None),
        P(("groups", "dp", "expert")),
        P(None, ("dp", "expert")),
        P(None, ("dp", "expert")),
        P(("dp", "expert"), None),
    )
    n_dp = mesh.shape["dp"]
    two_groups = n_dp == E and mesh.shape["expert"] == 2 and mesh.shape["groups"] == 2
    return jax.shard_map(
        functools.partial(fused, n_dp) if two_groups else on_device,
        mesh=mesh,
        in_specs=placed,
        out_specs=(
            P(("groups", "dp", "expert"), None),
            P(("groups", "dp", "expert"), None),
            P(("groups", "dp", "expert"), None),
        ),
        check_vma=False,
    )
```

```python
import functools

import jax
import jax.numpy as jnp
from jax import lax
from jax.experimental import pallas as pl
from jax.experimental.pallas import tpu as pltpu
from jax.sharding import PartitionSpec as P

E = 8
X_CUTS = (2048, 2048)
OUT_CUTS = (4096,)
GRAD_CUTS = (1024, 1024, 1024, 1024)
ROWS_IN = 512
TILE = 16
NN = (((1,), (0,)), ((), ()))
NT = (((1,), (1,)), ((), ()))


def expert_rows(got_x, got_dy, got_w, gate_weight, up_weight, down_weight):
    gate_pre = jnp.dot(got_x, gate_weight, preferred_element_type=jnp.float32)
    up_pre = jnp.dot(got_x, up_weight, preferred_element_type=jnp.float32)
    sig_gate = jax.nn.sigmoid(gate_pre)
    silu_gate = gate_pre * sig_gate
    hidden = (silu_gate * up_pre).astype(jnp.bfloat16)
    part_out = jnp.dot(hidden, down_weight, preferred_element_type=jnp.float32)
    d_hidden = got_w[:, None] * jnp.dot(got_dy, down_weight.T, preferred_element_type=jnp.float32)
    d_gate = (d_hidden * up_pre * sig_gate * (1.0 + gate_pre * (1.0 - sig_gate))).astype(
        jnp.bfloat16
    )
    d_up = (d_hidden * silu_gate).astype(jnp.bfloat16)
    part_grad = jnp.dot(d_gate, gate_weight.T, preferred_element_type=jnp.float32)
    part_grad = part_grad + jnp.dot(d_up, up_weight.T, preferred_element_type=jnp.float32)
    return (part_out.astype(jnp.bfloat16), part_grad.astype(jnp.bfloat16))


def on_device(tokens, cotangent, routing, gate_first, gate_weight, up_weight, down_weight):
    devices = lax.axis_size(("dp", "expert"))
    group_size = devices // E
    tok_rows = tokens.shape[0]
    width = tokens.shape[1]
    capacity = tok_rows // 2
    expert_ids = jnp.arange(E, dtype=jnp.int32)
    first_hot = (routing[:, 0:1] == expert_ids[None, :]).astype(jnp.int32)
    second_hot = (routing[:, 1:2] == expert_ids[None, :]).astype(jnp.int32)
    hot = first_hot + second_hot
    row_ids = jnp.arange(tok_rows, dtype=jnp.int32)
    not_later = (row_ids[:, None] >= row_ids[None, :]).astype(jnp.int32)
    rank_rows = jnp.sum(not_later[:, :, None] * hot[None, :, :], axis=1) - 1
    slot_ids = jnp.arange(capacity, dtype=jnp.int32)
    slot_hot = (rank_rows[:, :, None] == slot_ids[None, None, :]).astype(jnp.float32)
    pick_first = first_hot[:, :, None].astype(jnp.float32) * slot_hot
    pick_second = second_hot[:, :, None].astype(jnp.float32) * slot_hot
    picked = pick_first + pick_second
    share_first = gate_first.astype(jnp.float32) / 1024.0
    share_second = (1024 - gate_first).astype(jnp.float32) / 1024.0
    picked_low = picked.astype(jnp.bfloat16)
    send_x = jnp.einsum(
        "tec,td->ecd", picked_low, tokens, preferred_element_type=jnp.float32
    ).astype(jnp.bfloat16)
    send_dy = jnp.einsum(
        "tec,td->ecd", picked_low, cotangent, preferred_element_type=jnp.float32
    ).astype(jnp.bfloat16)
    weighted = pick_first * share_first[:, None, None] + pick_second * share_second[:, None, None]
    send_w = jnp.sum(weighted, axis=0)
    out_x = jnp.repeat(send_x, group_size, axis=0)
    out_dy = jnp.repeat(send_dy, group_size, axis=0)
    out_w = jnp.repeat(send_w, group_size, axis=0)

    def exchange(value):
        return lax.all_to_all(value, ("dp", "expert"), split_axis=0, concat_axis=0, tiled=True)

    recv_x, recv_dy = exchange(out_x), exchange(out_dy)
    recv_w = exchange(out_w.astype(jnp.bfloat16)).astype(out_w.dtype)
    got_x = recv_x.reshape(devices * capacity, width)
    got_dy = recv_dy.reshape(devices * capacity, width)
    got_w = recv_w.reshape(devices * capacity)
    part_out, part_grad = expert_rows(got_x, got_dy, got_w, gate_weight, up_weight, down_weight)
    back_out = exchange(part_out.reshape(devices, capacity, width))
    back_grad = exchange(part_grad.reshape(devices, capacity, width))
    summed_out = jnp.sum(
        back_out.astype(jnp.float32).reshape(E, group_size, capacity, width), axis=1
    )
    summed_grad = jnp.sum(
        back_grad.astype(jnp.float32).reshape(E, group_size, capacity, width), axis=1
    )
    rank_first = jnp.take_along_axis(rank_rows, routing[:, 0:1], axis=1)[:, 0]
    rank_second = jnp.take_along_axis(rank_rows, routing[:, 1:2], axis=1)[:, 0]
    slot_first = routing[:, 0] * capacity + rank_first
    slot_second = routing[:, 1] * capacity + rank_second
    flat_out = summed_out.reshape(E * capacity, width)
    flat_grad = summed_grad.reshape(E * capacity, width)
    out_first = jnp.take(flat_out, slot_first, axis=0)
    out_second = jnp.take(flat_out, slot_second, axis=0)
    mixed = (share_first[:, None] * out_first + share_second[:, None] * out_second).astype(
        jnp.bfloat16
    )
    token_grad = (
        jnp.take(flat_grad, slot_first, axis=0) + jnp.take(flat_grad, slot_second, axis=0)
    ).astype(jnp.bfloat16)
    cot_float = cotangent.astype(jnp.float32)
    grad_first = jnp.sum(cot_float * out_first, axis=1)
    grad_second = jnp.sum(cot_float * out_second, axis=1)
    gate_grad = jnp.stack([grad_first, grad_second], axis=1)
    return (mixed, token_grad, gate_grad)


def spans(cuts, width):
    scale = width // sum(cuts)
    found, start = [], 0
    for cut in cuts:
        found.append((start, cut * scale))
        start += cut * scale
    return found


def one_hot(rows, columns, test):
    row = lax.broadcasted_iota(jnp.int32, (rows, columns), 0)
    col = lax.broadcasted_iota(jnp.int32, (rows, columns), 1)
    return jnp.where(test(row, col), 1.0, 0.0).astype(jnp.bfloat16)


def layer_kernel(
    n_dp,
    route_ref,
    first_ref,
    x_ref,
    dy_ref,
    gate_hbm,
    up_hbm,
    down_hbm,
    mixed_ref,
    grad_ref,
    score_ref,
    wide,
    down,
    both8,
    cot8,
    xs,
    dys,
    pre,
    hid,
    d_both,
    acc,
    pair_send,
    pair_recv,
    kept,
    side_send,
    side_recv,
    w_sem,
    in_sems,
    pass_sems,
    ring_sems,
    back_sems,
    packs,
    recvs,
    back_sends,
    back_recvs,
):
    tok, width = x_ref.shape
    cap = tok // 2
    segs = TILE // cap
    quarter = n_dp * cap
    rows = 4 * quarter
    lines = n_dp * TILE
    hidden = down_hbm.shape[0]
    part = hidden // 2
    grp = lax.axis_index("groups")
    dp = lax.axis_index("dp")
    core = lax.axis_index("expert")
    far, other = 1 - grp, 1 - core
    f32, bf16 = jnp.float32, jnp.bfloat16
    first_unit = pl.multiple_of(grp * part, part)

    def place(g, q, c):
        return {"groups": g, "dp": q, "expert": c}

    def remote(src, dst, send, arrive, where):
        return pltpu.make_async_remote_copy(
            src_ref=src,
            dst_ref=dst,
            send_sem=send,
            recv_sem=arrive,
            device_id=where,
            device_id_type=pl.DeviceIdType.MESH,
        )

    barrier = pltpu.get_barrier_semaphore()
    for where in [place(grp, lax.rem(dp + k, n_dp), core) for k in range(1, n_dp)] + [
        place(grp, dp, other),
        place(far, dp, core),
    ]:
        pl.semaphore_signal(
            barrier, inc=1, device_id=where, device_id_type=pl.DeviceIdType.MESH
        )

    wide_loads, down_loads = [], []
    for n in range(width // ROWS_IN):
        at = pl.ds(n * ROWS_IN, ROWS_IN)
        for m, ref in ((0, gate_hbm), (1, up_hbm)):
            wide_loads.append(
                pltpu.make_async_copy(
                    ref.at[at, pl.ds(first_unit, part)],
                    wide.at[at, pl.ds(m * part, part)],
                    w_sem.at[2 * n + m],
                )
            )
    for n in range(part // ROWS_IN):
        down_loads.append(
            pltpu.make_async_copy(
                down_hbm.at[pl.ds(first_unit + n * ROWS_IN, ROWS_IN), :],
                down.at[pl.ds(n * ROWS_IN, ROWS_IN), :],
                w_sem.at[2 * (width // ROWS_IN) + n],
            )
        )
    for copy in wide_loads + down_loads:
        copy.start()

    slots = []
    for t in range(tok):
        row = []
        for j in range(2):
            e = route_ref[j, t]
            rank = jnp.int32(0)
            for s in range(t):
                rank = rank + jnp.where((route_ref[0, s] == e) | (route_ref[1, s] == e), 1, 0)
            row.append(e * cap + rank)
        slots.append(row)

    x32, dy32 = x_ref[...].astype(f32), dy_ref[...].astype(f32)
    both8[0:tok, :] = x32
    both8[tok : 2 * tok, :] = dy32
    cot8[0:tok, :] = dy32
    cot8[tok : 2 * tok, :] = dy32

    def chosen_rows(offset):
        def test(row, col):
            hit = None
            for t in range(tok):
                mine = (row // segs == slots[t][0]) | (row // segs == slots[t][1])
                mine = mine & (col % (2 * tok) == offset + t)
                hit = mine if hit is None else hit | mine
            return hit & (row % segs == col // (2 * tok))

        return one_hot(lines, segs * 2 * tok, test)

    batches = [(0, start, size) for start, size in spans(X_CUTS, width)] + [(1, 0, width)]
    pick_rows = (chosen_rows(0), chosen_rows(tok))
    sends = []

    def pack(n):
        which, start, size = batches[n]
        step = size // segs
        stacked = jnp.concatenate(
            [both8[:, start + s * step : start + (s + 1) * step] for s in range(segs)], axis=0
        ).astype(bf16)
        lined = lax.dot_general(pick_rows[which], stacked, NN, preferred_element_type=f32)
        packs[n][...] = lined.astype(bf16).reshape(n_dp, TILE, step)

    def send(n):
        for k in range(1, n_dp):
            q = lax.rem(dp + k, n_dp)
            copy = remote(
                packs[n].at[q],
                recvs[n].at[grp, core, dp],
                in_sems.at[0, n, k],
                in_sems.at[1, n, k],
                place(grp, q, core),
            )
            copy.start()
            sends.append(copy)
        recvs[n][grp, core, dp] = packs[n][dp]

    pack(0)
    pl.semaphore_wait(barrier, n_dp + 1)
    send(0)
    pack(1)
    send(1)
    pack(2)

    def alone(body):
        pl.when(dp >= 0)(body)

    to_pair, to_far, pair_on = {}, {}, {}

    def pass_on(n):
        for k in range(1, n_dp):
            sends[n * (n_dp - 1) + k - 1].wait_recv()
        mine = recvs[n].at[grp, core]
        to_far[n] = remote(
            mine, mine, pass_sems.at[0, n], pass_sems.at[1, n], place(far, dp, core)
        )
        to_pair[n] = remote(
            mine, mine, pass_sems.at[2, n], pass_sems.at[3, n], place(grp, dp, other)
        )
        to_far[n].start()
        to_pair[n].start()

    def pass_far(n):
        to_far[n].wait_recv()
        theirs = recvs[n].at[far, core]
        pair_on[n] = remote(
            theirs, theirs, pass_sems.at[4, n], pass_sems.at[5, n], place(grp, dp, other)
        )
        pair_on[n].start()

    unmix = one_hot(
        lines, lines, lambda row, col: (row // quarter == col % segs) & (row % quarter == col // segs)
    )
    mix = one_hot(
        lines, lines, lambda row, col: (col // quarter == row % segs) & (col % quarter == row // segs)
    )

    def unpack(n, dest):
        which, start, size = batches[n]
        step = size // segs
        to_pair[n].wait_recv()
        pair_on[n].wait_recv()
        for g in range(2):
            for c in range(2):
                lined = recvs[n][g, c].reshape(lines, step)
                flat = lax.dot_general(unmix, lined, NN, preferred_element_type=f32).astype(bf16)
                top = (2 * g + c) * quarter
                for s in range(segs):
                    dest[top : top + quarter, start + s * step : start + (s + 1) * step] = flat[
                        s * quarter : (s + 1) * quarter, :
                    ]

    def multiply_in(n, between):
        _, start, size = batches[n]
        for m in range(start // ROWS_IN, (start + size) // ROWS_IN):
            wide_loads[2 * m].wait()
            wide_loads[2 * m + 1].wait()
        block = 2 * part // 4

        def some(first, end):
            for m in range(first, end):
                cols = slice(m * block, (m + 1) * block)
                term = lax.dot_general(
                    xs[:, start : start + size],
                    wide[start : start + size, cols],
                    NN,
                    preferred_element_type=f32,
                )
                pre[:, cols] = term if n == 0 else pre[:, cols] + term

        alone(lambda: some(0, 2))
        between()
        alone(lambda: some(2, 4))

    def first_between():
        pass_on(2)
        pass_far(1)

    pass_on(0)
    send(2)
    pass_on(1)
    pass_far(0)
    unpack(0, xs)
    multiply_in(0, first_between)
    unpack(1, xs)
    multiply_in(1, lambda: pass_far(2))
    unpack(2, dys)
    for copy in down_loads:
        copy.wait()

    block = part // 4
    for m in range(4):
        cols = slice(m * block, (m + 1) * block)
        more = slice(part + m * block, part + (m + 1) * block)
        d_hidden = lax.dot_general(down[cols, :], dys[...], NT, preferred_element_type=f32).T
        gate_pre, up_pre = pre[:, cols], pre[:, more]
        sig = 1.0 / (1.0 + jnp.exp(-gate_pre))
        silu = gate_pre * sig
        hid[:, cols] = (silu * up_pre).astype(bf16)
        d_both[:, cols] = (d_hidden * up_pre * sig * (1.0 + gate_pre * (1.0 - sig))).astype(bf16)
        d_both[:, more] = (d_hidden * silu).astype(bf16)

    items = [(0, start, size) for start, size in spans(OUT_CUTS, width)]
    items += [(1, start, size) for start, size in spans(GRAD_CUTS, width)]
    pair_copies, side_copies, home_copies = {}, {}, {}

    def compute(i):
        which, start, size = items[i]
        cols = slice(start, start + size)

        def multiply():
            if which == 1:
                acc[1, :, cols] = lax.dot_general(
                    wide[cols, :], d_both[...], NT, preferred_element_type=f32
                ).T
                return
            block = min(size, 1024)
            for at in range(start, start + size, block):
                acc[0, :, at : at + block] = lax.dot_general(
                    hid[...], down[:, at : at + block], NN, preferred_element_type=f32
                )

        alone(multiply)
        for g in range(2):
            give = pl.ds(pl.multiple_of((2 * g + other) * quarter, quarter), quarter)
            pair_send[which, g, :, cols] = acc[which, give, cols].astype(bf16)
        pair_copies[i] = remote(
            pair_send.at[which, :, :, pl.ds(start, size)],
            pair_recv.at[which, :, :, pl.ds(start, size)],
            ring_sems.at[0, i],
            ring_sems.at[1, i],
            place(grp, dp, other),
        )
        pair_copies[i].start()

    def to_side(i):
        which, start, size = items[i]
        cols = slice(start, start + size)
        pair_copies[i].wait_recv()

        def total(g):
            own = pl.ds(pl.multiple_of((2 * g + core) * quarter, quarter), quarter)
            return acc[which, own, cols] + pair_recv[which, g, :, cols].astype(f32)

        side_send[which, :, cols] = total(far).astype(bf16)
        side_copies[i] = remote(
            side_send.at[which, :, pl.ds(start, size)],
            side_recv.at[which, :, pl.ds(start, size)],
            ring_sems.at[2, i],
            ring_sems.at[3, i],
            place(far, dp, core),
        )
        side_copies[i].start()
        kept[which, :, cols] = total(grp)

    def to_home(i):
        which, start, size = items[i]
        step = size // segs
        side_copies[i].wait_recv()
        cols = slice(start, start + size)
        total = (kept[which, :, cols] + side_recv[which, :, cols].astype(f32)).astype(bf16)
        stacked = jnp.concatenate([total[:, s * step : (s + 1) * step] for s in range(segs)], axis=0)
        lined = lax.dot_general(mix, stacked, NN, preferred_element_type=f32).astype(bf16)
        back_sends[i][...] = lined.reshape(n_dp, TILE, step)
        home_copies[i] = []
        for k in range(1, n_dp):
            q = lax.rem(dp + k, n_dp)
            copy = remote(
                back_sends[i].at[q],
                back_recvs[i].at[dp],
                back_sems.at[0, i, k],
                back_sems.at[1, i, k],
                place(grp, q, core),
            )
            copy.start()
            home_copies[i].append(copy)
        back_recvs[i][dp] = back_sends[i][dp]

    def pick_test(row, col):
        hit = None
        for t in range(tok):
            for j in range(2):
                mine = (row % (2 * tok) == j * tok + t) & (col // segs == slots[t][j])
                hit = mine if hit is None else hit | mine
        return hit & (row // (2 * tok) == col % segs)

    pick = one_hot(segs * 2 * tok, lines, pick_test)
    share_rows = lax.broadcasted_iota(jnp.int32, (2 * tok, 1), 0)
    units = jnp.zeros((2 * tok, 1), jnp.int32)
    for t in range(tok):
        units = jnp.where(share_rows == t, first_ref[t], units)
        units = jnp.where(share_rows == tok + t, 1024 - first_ref[t], units)
    share = units.astype(f32) / 1024.0
    scores = []

    def finish(i):
        which, start, size = items[i]
        step = size // segs
        for copy in home_copies[i]:
            copy.wait_recv()
        got = lax.dot_general(
            pick, back_recvs[i][...].reshape(lines, step), NN, preferred_element_type=f32
        )
        for s in range(segs):
            cols = slice(start + s * step, start + (s + 1) * step)
            here = got[s * 2 * tok : (s + 1) * 2 * tok, :]
            weighted = here * share
            summed = (weighted[:tok] + weighted[tok:]).astype(bf16)
            if which == 0:
                mixed_ref[:, cols] = summed
                scores.append(jnp.sum(here * cot8[:, cols], axis=1, keepdims=True))
            else:
                grad_ref[:, cols] = summed

    compute(0)
    compute(1)
    to_side(0)
    compute(2)
    to_side(1)
    compute(3)
    to_home(0)
    to_side(2)
    to_home(1)
    compute(4)
    to_side(3)
    to_home(2)

    to_side(4)
    to_home(3)
    finish(0)

    finish(1)
    to_home(4)
    finish(2)

    for i in range(3, len(items)):
        finish(i)

    score = scores[0]
    for more in scores[1:]:
        score = score + more
    row = lax.broadcasted_iota(jnp.int32, (2 * tok, tok), 0)
    col = lax.broadcasted_iota(jnp.int32, (2 * tok, tok), 1)
    for j in range(2):
        score_ref[j : j + 1, :] = jnp.sum(
            jnp.where(row == col + j * tok, score, 0.0), axis=0, keepdims=True
        )

    for copy in sends:
        copy.wait_send()
    for copies in (to_far, to_pair, pair_on, pair_copies, side_copies):
        for copy in copies.values():
            copy.wait_send()
    for copies in home_copies.values():
        for copy in copies:
            copy.wait_send()


def place_kernel(mixed_in, grad_in, score_in, mixed_out, grad_out, score_out):
    mixed_out[...] = mixed_in[...]
    grad_out[...] = grad_in[...]
    score_out[...] = score_in[...]


def fused(n_dp, tokens, cotangent, routing, gate_first, gate_weight, up_weight, down_weight):
    tok, width = tokens.shape
    cap = tok // 2
    segs = TILE // cap
    quarter = n_dp * cap
    rows = 4 * quarter
    hidden = down_weight.shape[0]
    part = hidden // 2
    f32, bf16 = jnp.float32, jnp.bfloat16
    vmem = pl.BlockSpec(memory_space=pltpu.VMEM)
    smem = pl.BlockSpec(memory_space=pltpu.SMEM)
    hbm = pl.BlockSpec(memory_space=pl.ANY)
    dma = pltpu.SemaphoreType.DMA
    steps_in = [size // segs for _, size in spans(X_CUTS, width)] + [width // segs]
    steps_out = [size // segs for _, size in spans(OUT_CUTS, width) + spans(GRAD_CUTS, width)]
    shapes = (
        jax.ShapeDtypeStruct((tok, width), bf16),
        jax.ShapeDtypeStruct((tok, width), bf16),
        jax.ShapeDtypeStruct((2, tok), f32),
    )
    results = pl.pallas_call(
        functools.partial(layer_kernel, n_dp),
        out_shape=shapes,
        in_specs=[smem, smem, vmem, vmem, hbm, hbm, hbm],
        out_specs=(vmem, vmem, vmem),
        scratch_shapes=[
            pltpu.VMEM((width, 2 * part), bf16),
            pltpu.VMEM((part, width), bf16),
            pltpu.VMEM((2 * tok, width), f32),
            pltpu.VMEM((2 * tok, width), f32),
            pltpu.VMEM((rows, width), bf16),
            pltpu.VMEM((rows, width), bf16),
            pltpu.VMEM((rows, 2 * part), f32),
            pltpu.VMEM((rows, part), bf16),
            pltpu.VMEM((rows, 2 * part), bf16),
            pltpu.VMEM((2, rows, width), f32),
            pltpu.VMEM((2, 2, quarter, width), bf16),
            pltpu.VMEM((2, 2, quarter, width), bf16),
            pltpu.VMEM((2, quarter, width), f32),
            pltpu.VMEM((2, quarter, width), bf16),
            pltpu.VMEM((2, quarter, width), bf16),
            dma((2 * (width // ROWS_IN) + part // ROWS_IN,)),
            dma((2, len(steps_in), n_dp)),
            dma((6, len(steps_in))),
            dma((4, len(steps_out))),
            dma((2, len(steps_out), n_dp)),
            [pltpu.VMEM((n_dp, TILE, step), bf16) for step in steps_in],
            [pltpu.VMEM((2, 2, n_dp, TILE, step), bf16) for step in steps_in],
            [pltpu.VMEM((n_dp, TILE, step), bf16) for step in steps_out],
            [pltpu.VMEM((n_dp, TILE, step), bf16) for step in steps_out],
        ],
        compiler_params=pltpu.CompilerParams(
            collective_id=0, has_side_effects=True, vmem_limit_bytes=61 * 1024 * 1024
        ),
    )(routing.T, gate_first, tokens, cotangent, gate_weight, up_weight, down_weight)
    mixed, grad, score = pl.pallas_call(
        place_kernel,
        out_shape=shapes,
        in_specs=[vmem] * 3,
        out_specs=(vmem, vmem, vmem),
    )(*results)
    return mixed, grad, score.T


def solution(mesh):
    placed = (
        P(("groups", "dp", "expert"), None),
        P(("groups", "dp", "expert"), None),
        P(("groups", "dp", "expert"), None),
        P(("groups", "dp", "expert")),
        P(None, ("dp", "expert")),
        P(None, ("dp", "expert")),
        P(("dp", "expert"), None),
    )
    n_dp = mesh.shape["dp"]
    two_groups = n_dp == E and mesh.shape["expert"] == 2 and mesh.shape["groups"] == 2
    return jax.shard_map(
        functools.partial(fused, n_dp) if two_groups else on_device,
        mesh=mesh,
        in_specs=placed,
        out_specs=(
            P(("groups", "dp", "expert"), None),
            P(("groups", "dp", "expert"), None),
            P(("groups", "dp", "expert"), None),
        ),
        check_vma=False,
    )
```

```python
import functools

import jax
import jax.numpy as jnp
from jax import lax
from jax.experimental import pallas as pl
from jax.experimental.pallas import tpu as pltpu
from jax.sharding import PartitionSpec as P

E = 8
X_CUTS = (1024, 3072)
OUT_CUTS = (4096,)
GRAD_CUTS = (1024, 1024, 1024, 1024)
ROWS_IN = 512
TILE = 16
NN = (((1,), (0,)), ((), ()))
NT = (((1,), (1,)), ((), ()))


def expert_rows(got_x, got_dy, got_w, gate_weight, up_weight, down_weight):
    gate_pre = jnp.dot(got_x, gate_weight, preferred_element_type=jnp.float32)
    up_pre = jnp.dot(got_x, up_weight, preferred_element_type=jnp.float32)
    sig_gate = jax.nn.sigmoid(gate_pre)
    silu_gate = gate_pre * sig_gate
    hidden = (silu_gate * up_pre).astype(jnp.bfloat16)
    part_out = jnp.dot(hidden, down_weight, preferred_element_type=jnp.float32)
    d_hidden = got_w[:, None] * jnp.dot(got_dy, down_weight.T, preferred_element_type=jnp.float32)
    d_gate = (d_hidden * up_pre * sig_gate * (1.0 + gate_pre * (1.0 - sig_gate))).astype(
        jnp.bfloat16
    )
    d_up = (d_hidden * silu_gate).astype(jnp.bfloat16)
    part_grad = jnp.dot(d_gate, gate_weight.T, preferred_element_type=jnp.float32)
    part_grad = part_grad + jnp.dot(d_up, up_weight.T, preferred_element_type=jnp.float32)
    return (part_out.astype(jnp.bfloat16), part_grad.astype(jnp.bfloat16))


def on_device(tokens, cotangent, routing, gate_first, gate_weight, up_weight, down_weight):
    devices = lax.axis_size(("dp", "expert"))
    group_size = devices // E
    tok_rows = tokens.shape[0]
    width = tokens.shape[1]
    capacity = tok_rows // 2
    expert_ids = jnp.arange(E, dtype=jnp.int32)
    first_hot = (routing[:, 0:1] == expert_ids[None, :]).astype(jnp.int32)
    second_hot = (routing[:, 1:2] == expert_ids[None, :]).astype(jnp.int32)
    hot = first_hot + second_hot
    row_ids = jnp.arange(tok_rows, dtype=jnp.int32)
    not_later = (row_ids[:, None] >= row_ids[None, :]).astype(jnp.int32)
    rank_rows = jnp.sum(not_later[:, :, None] * hot[None, :, :], axis=1) - 1
    slot_ids = jnp.arange(capacity, dtype=jnp.int32)
    slot_hot = (rank_rows[:, :, None] == slot_ids[None, None, :]).astype(jnp.float32)
    pick_first = first_hot[:, :, None].astype(jnp.float32) * slot_hot
    pick_second = second_hot[:, :, None].astype(jnp.float32) * slot_hot
    picked = pick_first + pick_second
    share_first = gate_first.astype(jnp.float32) / 1024.0
    share_second = (1024 - gate_first).astype(jnp.float32) / 1024.0
    picked_low = picked.astype(jnp.bfloat16)
    send_x = jnp.einsum(
        "tec,td->ecd", picked_low, tokens, preferred_element_type=jnp.float32
    ).astype(jnp.bfloat16)
    send_dy = jnp.einsum(
        "tec,td->ecd", picked_low, cotangent, preferred_element_type=jnp.float32
    ).astype(jnp.bfloat16)
    weighted = pick_first * share_first[:, None, None] + pick_second * share_second[:, None, None]
    send_w = jnp.sum(weighted, axis=0)
    out_x = jnp.repeat(send_x, group_size, axis=0)
    out_dy = jnp.repeat(send_dy, group_size, axis=0)
    out_w = jnp.repeat(send_w, group_size, axis=0)

    def exchange(value):
        return lax.all_to_all(value, ("dp", "expert"), split_axis=0, concat_axis=0, tiled=True)

    recv_x, recv_dy = exchange(out_x), exchange(out_dy)
    recv_w = exchange(out_w.astype(jnp.bfloat16)).astype(out_w.dtype)
    got_x = recv_x.reshape(devices * capacity, width)
    got_dy = recv_dy.reshape(devices * capacity, width)
    got_w = recv_w.reshape(devices * capacity)
    part_out, part_grad = expert_rows(got_x, got_dy, got_w, gate_weight, up_weight, down_weight)
    back_out = exchange(part_out.reshape(devices, capacity, width))
    back_grad = exchange(part_grad.reshape(devices, capacity, width))
    summed_out = jnp.sum(
        back_out.astype(jnp.float32).reshape(E, group_size, capacity, width), axis=1
    )
    summed_grad = jnp.sum(
        back_grad.astype(jnp.float32).reshape(E, group_size, capacity, width), axis=1
    )
    rank_first = jnp.take_along_axis(rank_rows, routing[:, 0:1], axis=1)[:, 0]
    rank_second = jnp.take_along_axis(rank_rows, routing[:, 1:2], axis=1)[:, 0]
    slot_first = routing[:, 0] * capacity + rank_first
    slot_second = routing[:, 1] * capacity + rank_second
    flat_out = summed_out.reshape(E * capacity, width)
    flat_grad = summed_grad.reshape(E * capacity, width)
    out_first = jnp.take(flat_out, slot_first, axis=0)
    out_second = jnp.take(flat_out, slot_second, axis=0)
    mixed = (share_first[:, None] * out_first + share_second[:, None] * out_second).astype(
        jnp.bfloat16
    )
    token_grad = (
        jnp.take(flat_grad, slot_first, axis=0) + jnp.take(flat_grad, slot_second, axis=0)
    ).astype(jnp.bfloat16)
    cot_float = cotangent.astype(jnp.float32)
    grad_first = jnp.sum(cot_float * out_first, axis=1)
    grad_second = jnp.sum(cot_float * out_second, axis=1)
    gate_grad = jnp.stack([grad_first, grad_second], axis=1)
    return (mixed, token_grad, gate_grad)


def spans(cuts, width):
    scale = width // sum(cuts)
    found, start = [], 0
    for cut in cuts:
        found.append((start, cut * scale))
        start += cut * scale
    return found


def one_hot(rows, columns, test):
    row = lax.broadcasted_iota(jnp.int32, (rows, columns), 0)
    col = lax.broadcasted_iota(jnp.int32, (rows, columns), 1)
    return jnp.where(test(row, col), 1.0, 0.0).astype(jnp.bfloat16)


def layer_kernel(
    n_dp,
    route_hbm,
    first_hbm,
    x_hbm,
    dy_hbm,
    gate_hbm,
    up_hbm,
    down_hbm,
    mixed_ref,
    grad_ref,
    score_ref,
    route_ref,
    first_ref,
    x_ref,
    dy_ref,
    wide,
    down,
    both8,
    cot8,
    xs,
    dys,
    pre,
    hid,
    d_both,
    acc,
    pair_send,
    pair_recv,
    kept,
    side_send,
    side_recv,
    small_sems,
    w_sem,
    in_sems,
    pass_sems,
    ring_sems,
    back_sems,
    packs,
    recvs,
    back_sends,
    back_recvs,
):
    tok, width = x_ref.shape
    cap = tok // 2
    segs = TILE // cap
    quarter = n_dp * cap
    rows = 4 * quarter
    lines = n_dp * TILE
    hidden = down_hbm.shape[0]
    part = hidden // 2
    grp = lax.axis_index("groups")
    dp = lax.axis_index("dp")
    core = lax.axis_index("expert")
    far, other = 1 - grp, 1 - core
    f32, bf16 = jnp.float32, jnp.bfloat16
    first_unit = pl.multiple_of(grp * part, part)

    def place(g, q, c):
        return {"groups": g, "dp": q, "expert": c}

    def remote(src, dst, send, arrive, where):
        return pltpu.make_async_remote_copy(
            src_ref=src,
            dst_ref=dst,
            send_sem=send,
            recv_sem=arrive,
            device_id=where,
            device_id_type=pl.DeviceIdType.MESH,
        )

    barrier = pltpu.get_barrier_semaphore()
    for where in [place(grp, lax.rem(dp + k, n_dp), core) for k in range(1, n_dp)] + [
        place(grp, dp, other),
        place(far, dp, core),
    ]:
        pl.semaphore_signal(
            barrier, inc=1, device_id=where, device_id_type=pl.DeviceIdType.MESH
        )

    small_loads = [
        pltpu.make_async_copy(src, dst, small_sems.at[n])
        for n, (src, dst) in enumerate(
            ((route_hbm, route_ref), (first_hbm, first_ref), (x_hbm, x_ref), (dy_hbm, dy_ref))
        )
    ]
    for copy in small_loads:
        copy.start()
    wide_loads, down_loads = [], []
    for n in range(width // ROWS_IN):
        at = pl.ds(n * ROWS_IN, ROWS_IN)
        for m, ref in ((0, gate_hbm), (1, up_hbm)):
            wide_loads.append(
                pltpu.make_async_copy(
                    ref.at[at, pl.ds(first_unit, part)],
                    wide.at[at, pl.ds(m * part, part)],
                    w_sem.at[2 * n + m],
                )
            )
    for n in range(part // ROWS_IN):
        down_loads.append(
            pltpu.make_async_copy(
                down_hbm.at[pl.ds(first_unit + n * ROWS_IN, ROWS_IN), :],
                down.at[pl.ds(n * ROWS_IN, ROWS_IN), :],
                w_sem.at[2 * (width // ROWS_IN) + n],
            )
        )

    for copy in small_loads:
        copy.wait()
    first_loads = len(wide_loads) // 2
    for copy in wide_loads[:first_loads]:
        copy.start()
    slots = []
    for t in range(tok):
        row = []
        for j in range(2):
            e = route_ref[j, t]
            rank = jnp.int32(0)
            for s in range(t):
                rank = rank + jnp.where((route_ref[0, s] == e) | (route_ref[1, s] == e), 1, 0)
            row.append(e * cap + rank)
        slots.append(row)

    x32, dy32 = x_ref[...].astype(f32), dy_ref[...].astype(f32)
    both8[0:tok, :] = x32
    both8[tok : 2 * tok, :] = dy32
    cot8[0:tok, :] = dy32
    cot8[tok : 2 * tok, :] = dy32

    def chosen_rows(offset):
        def test(row, col):
            hit = None
            for t in range(tok):
                mine = (row // segs == slots[t][0]) | (row // segs == slots[t][1])
                mine = mine & (col % (2 * tok) == offset + t)
                hit = mine if hit is None else hit | mine
            return hit & (row % segs == col // (2 * tok))

        return one_hot(lines, segs * 2 * tok, test)

    batches = [(0, start, size) for start, size in spans(X_CUTS, width)] + [(1, 0, width)]
    pick_rows = (chosen_rows(0), chosen_rows(tok))
    sends = []

    def pack(n):
        which, start, size = batches[n]
        step = size // segs
        stacked = jnp.concatenate(
            [both8[:, start + s * step : start + (s + 1) * step] for s in range(segs)], axis=0
        ).astype(bf16)
        lined = lax.dot_general(pick_rows[which], stacked, NN, preferred_element_type=f32)
        packs[n][...] = lined.astype(bf16).reshape(n_dp, TILE, step)

    def send(n):
        for k in range(1, n_dp):
            q = lax.rem(dp + k, n_dp)
            copy = remote(
                packs[n].at[q],
                recvs[n].at[grp, core, dp],
                in_sems.at[0, n, k],
                in_sems.at[1, n, k],
                place(grp, q, core),
            )
            copy.start()
            sends.append(copy)
        recvs[n][grp, core, dp] = packs[n][dp]

    pack(0)
    pl.semaphore_wait(barrier, n_dp + 1)
    send(0)
    pack(1)
    send(1)
    for copy in wide_loads[first_loads:]:
        copy.start()
    pack(2)

    def alone(body):
        pl.when(dp >= 0)(body)

    to_pair, to_far, pair_on = {}, {}, {}

    def pass_on(n):
        for k in range(1, n_dp):
            sends[n * (n_dp - 1) + k - 1].wait_recv()
        mine = recvs[n].at[grp, core]
        to_far[n] = remote(
            mine, mine, pass_sems.at[0, n], pass_sems.at[1, n], place(far, dp, core)
        )
        to_pair[n] = remote(
            mine, mine, pass_sems.at[2, n], pass_sems.at[3, n], place(grp, dp, other)
        )
        to_far[n].start()
        to_pair[n].start()

    def pass_far(n):
        to_far[n].wait_recv()
        theirs = recvs[n].at[far, core]
        pair_on[n] = remote(
            theirs, theirs, pass_sems.at[4, n], pass_sems.at[5, n], place(grp, dp, other)
        )
        pair_on[n].start()

    unmix = one_hot(
        lines, lines, lambda row, col: (row // quarter == col % segs) & (row % quarter == col // segs)
    )
    mix = one_hot(
        lines, lines, lambda row, col: (col // quarter == row % segs) & (col % quarter == row // segs)
    )

    def unpack(n, dest):
        which, start, size = batches[n]
        step = size // segs
        to_pair[n].wait_recv()
        pair_on[n].wait_recv()
        for g in range(2):
            for c in range(2):
                lined = recvs[n][g, c].reshape(lines, step)
                flat = lax.dot_general(unmix, lined, NN, preferred_element_type=f32).astype(bf16)
                top = (2 * g + c) * quarter
                for s in range(segs):
                    dest[top : top + quarter, start + s * step : start + (s + 1) * step] = flat[
                        s * quarter : (s + 1) * quarter, :
                    ]

    def multiply_in(n, between):
        _, start, size = batches[n]
        for m in range(start // ROWS_IN, (start + size) // ROWS_IN):
            wide_loads[2 * m].wait()
            wide_loads[2 * m + 1].wait()
        block = 2 * part // 4

        def some(first, end):
            for m in range(first, end):
                cols = slice(m * block, (m + 1) * block)
                term = lax.dot_general(
                    xs[:, start : start + size],
                    wide[start : start + size, cols],
                    NN,
                    preferred_element_type=f32,
                )
                pre[:, cols] = term if n == 0 else pre[:, cols] + term

        alone(lambda: some(0, 2))
        between()
        alone(lambda: some(2, 4))

    def first_between():
        pass_far(1)

    pass_on(0)
    send(2)
    for copy in down_loads:
        copy.start()
    pass_on(1)
    pass_far(0)
    unpack(0, xs)
    multiply_in(0, first_between)
    pass_on(2)
    unpack(1, xs)
    multiply_in(1, lambda: None)
    for copy in down_loads:
        copy.wait()

    def gate(m):
        block = part // 4
        cols = slice(m * block, (m + 1) * block)
        more = slice(part + m * block, part + (m + 1) * block)
        gate_pre, up_pre = pre[:, cols], pre[:, more]
        sig = 1.0 / (1.0 + jnp.exp(-gate_pre))
        return cols, more, gate_pre, up_pre, sig, gate_pre * sig

    def forward():
        for m in range(4):
            cols, _, _, up_pre, _, silu = gate(m)
            hid[:, cols] = (silu * up_pre).astype(bf16)

    def backward():
        for m in range(4):
            cols, more, gate_pre, up_pre, sig, silu = gate(m)
            d_hidden = lax.dot_general(down[cols, :], dys[...], NT, preferred_element_type=f32).T
            d_both[:, cols] = (d_hidden * up_pre * sig * (1.0 + gate_pre * (1.0 - sig))).astype(bf16)
            d_both[:, more] = (d_hidden * silu).astype(bf16)

    alone(forward)

    items = [(0, start, size) for start, size in spans(OUT_CUTS, width)]
    items += [(1, start, size) for start, size in spans(GRAD_CUTS, width)]
    pair_copies, side_copies, home_copies = {}, {}, {}

    def compute(i, between=None):
        which, start, size = items[i]
        cols = slice(start, start + size)

        def multiply(first=start):
            if which == 1:
                acc[1, :, cols] = lax.dot_general(
                    wide[cols, :], d_both[...], NT, preferred_element_type=f32
                ).T
                return
            block = min(size, 1024)
            for at in range(first, first + size // 2, block):
                acc[0, :, at : at + block] = lax.dot_general(
                    hid[...], down[:, at : at + block], NN, preferred_element_type=f32
                )

        alone(multiply)
        if which == 0:
            between()
            alone(lambda: multiply(start + size // 2))
        for g in range(2):
            give = pl.ds(pl.multiple_of((2 * g + other) * quarter, quarter), quarter)
            pair_send[which, g, :, cols] = acc[which, give, cols].astype(bf16)
        pair_copies[i] = remote(
            pair_send.at[which, :, :, pl.ds(start, size)],
            pair_recv.at[which, :, :, pl.ds(start, size)],
            ring_sems.at[0, i],
            ring_sems.at[1, i],
            place(grp, dp, other),
        )
        pair_copies[i].start()

    def to_side(i):
        which, start, size = items[i]
        cols = slice(start, start + size)
        pair_copies[i].wait_recv()

        def total(g):
            own = pl.ds(pl.multiple_of((2 * g + core) * quarter, quarter), quarter)
            return acc[which, own, cols] + pair_recv[which, g, :, cols].astype(f32)

        side_send[which, :, cols] = total(far).astype(bf16)
        side_copies[i] = remote(
            side_send.at[which, :, pl.ds(start, size)],
            side_recv.at[which, :, pl.ds(start, size)],
            ring_sems.at[2, i],
            ring_sems.at[3, i],
            place(far, dp, core),
        )
        side_copies[i].start()
        kept[which, :, cols] = total(grp)

    def to_home(i):
        which, start, size = items[i]
        step = size // segs
        side_copies[i].wait_recv()
        cols = slice(start, start + size)
        total = (kept[which, :, cols] + side_recv[which, :, cols].astype(f32)).astype(bf16)
        stacked = jnp.concatenate([total[:, s * step : (s + 1) * step] for s in range(segs)], axis=0)
        lined = lax.dot_general(mix, stacked, NN, preferred_element_type=f32).astype(bf16)
        back_sends[i][...] = lined.reshape(n_dp, TILE, step)
        home_copies[i] = []
        for k in range(1, n_dp):
            q = lax.rem(dp + k, n_dp)
            copy = remote(
                back_sends[i].at[q],
                back_recvs[i].at[dp],
                back_sems.at[0, i, k],
                back_sems.at[1, i, k],
                place(grp, q, core),
            )
            copy.start()
            home_copies[i].append(copy)
        back_recvs[i][dp] = back_sends[i][dp]

    def pick_test(row, col):
        hit = None
        for t in range(tok):
            for j in range(2):
                mine = (row % (2 * tok) == j * tok + t) & (col // segs == slots[t][j])
                hit = mine if hit is None else hit | mine
        return hit & (row // (2 * tok) == col % segs)

    pick = one_hot(segs * 2 * tok, lines, pick_test)
    share_rows = lax.broadcasted_iota(jnp.int32, (2 * tok, 1), 0)
    units = jnp.zeros((2 * tok, 1), jnp.int32)
    for t in range(tok):
        units = jnp.where(share_rows == t, first_ref[t], units)
        units = jnp.where(share_rows == tok + t, 1024 - first_ref[t], units)
    share = units.astype(f32) / 1024.0
    scores = []

    def finish(i):
        which, start, size = items[i]
        step = size // segs
        for copy in home_copies[i]:
            copy.wait_recv()
        got = lax.dot_general(
            pick, back_recvs[i][...].reshape(lines, step), NN, preferred_element_type=f32
        )
        for s in range(segs):
            cols = slice(start + s * step, start + (s + 1) * step)
            here = got[s * 2 * tok : (s + 1) * 2 * tok, :]
            weighted = here * share
            summed = (weighted[:tok] + weighted[tok:]).astype(bf16)
            if which == 0:
                mixed_ref[:, cols] = summed
                scores.append(jnp.sum(here * cot8[:, cols], axis=1, keepdims=True))
            else:
                grad_ref[:, cols] = summed

    compute(0, lambda: pass_far(2))
    unpack(2, dys)
    to_side(0)
    alone(backward)
    compute(1)
    to_home(0)
    compute(2)
    to_side(1)
    compute(3)
    to_side(2)
    to_home(1)
    compute(4)
    to_side(3)
    to_home(2)
    to_side(4)
    finish(0)
    to_home(3)
    finish(1)
    to_home(4)
    finish(2)
    finish(3)
    for copy in sends:
        copy.wait_send()
    for copies in (to_far, to_pair, pair_on, pair_copies, side_copies):
        for copy in copies.values():
            copy.wait_send()
    for copies in home_copies.values():
        for copy in copies:
            copy.wait_send()
    finish(4)

    score = scores[0]
    for more in scores[1:]:
        score = score + more
    row = lax.broadcasted_iota(jnp.int32, (2 * tok, tok), 0)
    col = lax.broadcasted_iota(jnp.int32, (2 * tok, tok), 1)
    for j in range(2):
        score_ref[j : j + 1, :] = jnp.sum(
            jnp.where(row == col + j * tok, score, 0.0), axis=0, keepdims=True
        )


def place_kernel(mixed_in, grad_in, score_in, mixed_out, grad_out, score_out):
    mixed_out[...] = mixed_in[...]
    grad_out[...] = grad_in[...]
    score_out[...] = score_in[...]


def fused(n_dp, tokens, cotangent, routing, gate_first, gate_weight, up_weight, down_weight):
    tok, width = tokens.shape
    cap = tok // 2
    segs = TILE // cap
    quarter = n_dp * cap
    rows = 4 * quarter
    hidden = down_weight.shape[0]
    part = hidden // 2
    f32, bf16 = jnp.float32, jnp.bfloat16
    vmem = pl.BlockSpec(memory_space=pltpu.VMEM)
    hbm = pl.BlockSpec(memory_space=pl.ANY)
    dma = pltpu.SemaphoreType.DMA
    steps_in = [size // segs for _, size in spans(X_CUTS, width)] + [width // segs]
    steps_out = [size // segs for _, size in spans(OUT_CUTS, width) + spans(GRAD_CUTS, width)]
    shapes = (
        jax.ShapeDtypeStruct((tok, width), bf16),
        jax.ShapeDtypeStruct((tok, width), bf16),
        jax.ShapeDtypeStruct((2, tok), f32),
    )
    results = pl.pallas_call(
        functools.partial(layer_kernel, n_dp),
        out_shape=shapes,
        in_specs=[hbm] * 7,
        out_specs=(vmem, vmem, vmem),
        scratch_shapes=[
            pltpu.SMEM((2, tok), jnp.int32),
            pltpu.SMEM((tok,), jnp.int32),
            pltpu.VMEM((tok, width), bf16),
            pltpu.VMEM((tok, width), bf16),
            pltpu.VMEM((width, 2 * part), bf16),
            pltpu.VMEM((part, width), bf16),
            pltpu.VMEM((2 * tok, width), f32),
            pltpu.VMEM((2 * tok, width), f32),
            pltpu.VMEM((rows, width), bf16),
            pltpu.VMEM((rows, width), bf16),
            pltpu.VMEM((rows, 2 * part), f32),
            pltpu.VMEM((rows, part), bf16),
            pltpu.VMEM((rows, 2 * part), bf16),
            pltpu.VMEM((2, rows, width), f32),
            pltpu.VMEM((2, 2, quarter, width), bf16),
            pltpu.VMEM((2, 2, quarter, width), bf16),
            pltpu.VMEM((2, quarter, width), f32),
            pltpu.VMEM((2, quarter, width), bf16),
            pltpu.VMEM((2, quarter, width), bf16),
            dma((4,)),
            dma((2 * (width // ROWS_IN) + part // ROWS_IN,)),
            dma((2, len(steps_in), n_dp)),
            dma((6, len(steps_in))),
            dma((4, len(steps_out))),
            dma((2, len(steps_out), n_dp)),
            [pltpu.VMEM((n_dp, TILE, step), bf16) for step in steps_in],
            [pltpu.VMEM((2, 2, n_dp, TILE, step), bf16) for step in steps_in],
            [pltpu.VMEM((n_dp, TILE, step), bf16) for step in steps_out],
            [pltpu.VMEM((n_dp, TILE, step), bf16) for step in steps_out],
        ],
        compiler_params=pltpu.CompilerParams(
            collective_id=0, has_side_effects=True, vmem_limit_bytes=61 * 1024 * 1024
        ),
    )(routing.T, gate_first, tokens, cotangent, gate_weight, up_weight, down_weight)
    mixed, grad, score = pl.pallas_call(
        place_kernel,
        out_shape=shapes,
        in_specs=[vmem] * 3,
        out_specs=(vmem, vmem, vmem),
    )(*results)
    return mixed, grad, score.T


def solution(mesh):
    placed = (
        P(("groups", "dp", "expert"), None),
        P(("groups", "dp", "expert"), None),
        P(("groups", "dp", "expert"), None),
        P(("groups", "dp", "expert")),
        P(None, ("dp", "expert")),
        P(None, ("dp", "expert")),
        P(("dp", "expert"), None),
    )
    n_dp = mesh.shape["dp"]
    two_groups = n_dp == E and mesh.shape["expert"] == 2 and mesh.shape["groups"] == 2
    return jax.shard_map(
        functools.partial(fused, n_dp) if two_groups else on_device,
        mesh=mesh,
        in_specs=placed,
        out_specs=(
            P(("groups", "dp", "expert"), None),
            P(("groups", "dp", "expert"), None),
            P(("groups", "dp", "expert"), None),
        ),
        check_vma=False,
    )
```

```python
import functools

import jax
import jax.numpy as jnp
from jax import lax
from jax.experimental import pallas as pl
from jax.experimental.pallas import tpu as pltpu
from jax.sharding import PartitionSpec as P

E = 8
X_CUTS = (1024, 3072)
OUT_CUTS = (4096,)
GRAD_CUTS = (1536, 1024, 1024, 512)
ROWS_IN = 512
TILE = 16
NN = (((1,), (0,)), ((), ()))
NT = (((1,), (1,)), ((), ()))


def expert_rows(got_x, got_dy, got_w, gate_weight, up_weight, down_weight):
    gate_pre = jnp.dot(got_x, gate_weight, preferred_element_type=jnp.float32)
    up_pre = jnp.dot(got_x, up_weight, preferred_element_type=jnp.float32)
    sig_gate = jax.nn.sigmoid(gate_pre)
    silu_gate = gate_pre * sig_gate
    hidden = (silu_gate * up_pre).astype(jnp.bfloat16)
    part_out = jnp.dot(hidden, down_weight, preferred_element_type=jnp.float32)
    d_hidden = got_w[:, None] * jnp.dot(got_dy, down_weight.T, preferred_element_type=jnp.float32)
    d_gate = (d_hidden * up_pre * sig_gate * (1.0 + gate_pre * (1.0 - sig_gate))).astype(
        jnp.bfloat16
    )
    d_up = (d_hidden * silu_gate).astype(jnp.bfloat16)
    part_grad = jnp.dot(d_gate, gate_weight.T, preferred_element_type=jnp.float32)
    part_grad = part_grad + jnp.dot(d_up, up_weight.T, preferred_element_type=jnp.float32)
    return (part_out.astype(jnp.bfloat16), part_grad.astype(jnp.bfloat16))


def on_device(tokens, cotangent, routing, gate_first, gate_weight, up_weight, down_weight):
    devices = lax.axis_size(("dp", "expert"))
    group_size = devices // E
    tok_rows = tokens.shape[0]
    width = tokens.shape[1]
    capacity = tok_rows // 2
    expert_ids = jnp.arange(E, dtype=jnp.int32)
    first_hot = (routing[:, 0:1] == expert_ids[None, :]).astype(jnp.int32)
    second_hot = (routing[:, 1:2] == expert_ids[None, :]).astype(jnp.int32)
    hot = first_hot + second_hot
    row_ids = jnp.arange(tok_rows, dtype=jnp.int32)
    not_later = (row_ids[:, None] >= row_ids[None, :]).astype(jnp.int32)
    rank_rows = jnp.sum(not_later[:, :, None] * hot[None, :, :], axis=1) - 1
    slot_ids = jnp.arange(capacity, dtype=jnp.int32)
    slot_hot = (rank_rows[:, :, None] == slot_ids[None, None, :]).astype(jnp.float32)
    pick_first = first_hot[:, :, None].astype(jnp.float32) * slot_hot
    pick_second = second_hot[:, :, None].astype(jnp.float32) * slot_hot
    picked = pick_first + pick_second
    share_first = gate_first.astype(jnp.float32) / 1024.0
    share_second = (1024 - gate_first).astype(jnp.float32) / 1024.0
    picked_low = picked.astype(jnp.bfloat16)
    send_x = jnp.einsum(
        "tec,td->ecd", picked_low, tokens, preferred_element_type=jnp.float32
    ).astype(jnp.bfloat16)
    send_dy = jnp.einsum(
        "tec,td->ecd", picked_low, cotangent, preferred_element_type=jnp.float32
    ).astype(jnp.bfloat16)
    weighted = pick_first * share_first[:, None, None] + pick_second * share_second[:, None, None]
    send_w = jnp.sum(weighted, axis=0)
    out_x = jnp.repeat(send_x, group_size, axis=0)
    out_dy = jnp.repeat(send_dy, group_size, axis=0)
    out_w = jnp.repeat(send_w, group_size, axis=0)

    def exchange(value):
        return lax.all_to_all(value, ("dp", "expert"), split_axis=0, concat_axis=0, tiled=True)

    recv_x, recv_dy = exchange(out_x), exchange(out_dy)
    recv_w = exchange(out_w.astype(jnp.bfloat16)).astype(out_w.dtype)
    got_x = recv_x.reshape(devices * capacity, width)
    got_dy = recv_dy.reshape(devices * capacity, width)
    got_w = recv_w.reshape(devices * capacity)
    part_out, part_grad = expert_rows(got_x, got_dy, got_w, gate_weight, up_weight, down_weight)
    back_out = exchange(part_out.reshape(devices, capacity, width))
    back_grad = exchange(part_grad.reshape(devices, capacity, width))
    summed_out = jnp.sum(
        back_out.astype(jnp.float32).reshape(E, group_size, capacity, width), axis=1
    )
    summed_grad = jnp.sum(
        back_grad.astype(jnp.float32).reshape(E, group_size, capacity, width), axis=1
    )
    rank_first = jnp.take_along_axis(rank_rows, routing[:, 0:1], axis=1)[:, 0]
    rank_second = jnp.take_along_axis(rank_rows, routing[:, 1:2], axis=1)[:, 0]
    slot_first = routing[:, 0] * capacity + rank_first
    slot_second = routing[:, 1] * capacity + rank_second
    flat_out = summed_out.reshape(E * capacity, width)
    flat_grad = summed_grad.reshape(E * capacity, width)
    out_first = jnp.take(flat_out, slot_first, axis=0)
    out_second = jnp.take(flat_out, slot_second, axis=0)
    mixed = (share_first[:, None] * out_first + share_second[:, None] * out_second).astype(
        jnp.bfloat16
    )
    token_grad = (
        jnp.take(flat_grad, slot_first, axis=0) + jnp.take(flat_grad, slot_second, axis=0)
    ).astype(jnp.bfloat16)
    cot_float = cotangent.astype(jnp.float32)
    grad_first = jnp.sum(cot_float * out_first, axis=1)
    grad_second = jnp.sum(cot_float * out_second, axis=1)
    gate_grad = jnp.stack([grad_first, grad_second], axis=1)
    return (mixed, token_grad, gate_grad)


def spans(cuts, width):
    scale = width // sum(cuts)
    found, start = [], 0
    for cut in cuts:
        found.append((start, cut * scale))
        start += cut * scale
    return found


def one_hot(rows, columns, test):
    row = lax.broadcasted_iota(jnp.int32, (rows, columns), 0)
    col = lax.broadcasted_iota(jnp.int32, (rows, columns), 1)
    return jnp.where(test(row, col), 1.0, 0.0).astype(jnp.bfloat16)


def layer_kernel(
    n_dp,
    route_hbm,
    first_hbm,
    x_hbm,
    dy_hbm,
    gate_hbm,
    up_hbm,
    down_hbm,
    mixed_ref,
    grad_ref,
    score_ref,
    route_ref,
    first_ref,
    x_ref,
    dy_ref,
    wide,
    down,
    both8,
    cot8,
    xs,
    dys,
    pre,
    hid,
    d_both,
    acc,
    pair_send,
    pair_recv,
    kept,
    side_send,
    side_recv,
    small_sems,
    w_sem,
    in_sems,
    pass_sems,
    ring_sems,
    back_sems,
    packs,
    recvs,
    back_sends,
    back_recvs,
):
    tok, width = x_ref.shape
    cap = tok // 2
    segs = TILE // cap
    quarter = n_dp * cap
    rows = 4 * quarter
    lines = n_dp * TILE
    hidden = down_hbm.shape[0]
    part = hidden // 2
    grp = lax.axis_index("groups")
    dp = lax.axis_index("dp")
    core = lax.axis_index("expert")
    far, other = 1 - grp, 1 - core
    f32, bf16 = jnp.float32, jnp.bfloat16
    first_unit = pl.multiple_of(grp * part, part)

    def place(g, q, c):
        return {"groups": g, "dp": q, "expert": c}

    def remote(src, dst, send, arrive, where):
        return pltpu.make_async_remote_copy(
            src_ref=src,
            dst_ref=dst,
            send_sem=send,
            recv_sem=arrive,
            device_id=where,
            device_id_type=pl.DeviceIdType.MESH,
        )

    barrier = pltpu.get_barrier_semaphore()
    for where in [place(grp, lax.rem(dp + k, n_dp), core) for k in range(1, n_dp)] + [
        place(grp, dp, other),
        place(far, dp, core),
    ]:
        pl.semaphore_signal(
            barrier, inc=1, device_id=where, device_id_type=pl.DeviceIdType.MESH
        )

    small_loads = [
        pltpu.make_async_copy(src, dst, small_sems.at[n])
        for n, (src, dst) in enumerate(
            ((route_hbm, route_ref), (first_hbm, first_ref), (x_hbm, x_ref), (dy_hbm, dy_ref))
        )
    ]
    for copy in small_loads:
        copy.start()
    wide_loads, down_loads = [], []
    for n in range(width // ROWS_IN):
        at = pl.ds(n * ROWS_IN, ROWS_IN)
        for m, ref in ((0, gate_hbm), (1, up_hbm)):
            wide_loads.append(
                pltpu.make_async_copy(
                    ref.at[at, pl.ds(first_unit, part)],
                    wide.at[at, pl.ds(m * part, part)],
                    w_sem.at[2 * n + m],
                )
            )
    for n in range(part // ROWS_IN):
        down_loads.append(
            pltpu.make_async_copy(
                down_hbm.at[pl.ds(first_unit + n * ROWS_IN, ROWS_IN), :],
                down.at[pl.ds(n * ROWS_IN, ROWS_IN), :],
                w_sem.at[2 * (width // ROWS_IN) + n],
            )
        )

    for copy in small_loads:
        copy.wait()
    first_loads = len(wide_loads) // 2
    for copy in wide_loads[:first_loads]:
        copy.start()
    slots = []
    for t in range(tok):
        row = []
        for j in range(2):
            e = route_ref[j, t]
            rank = jnp.int32(0)
            for s in range(t):
                rank = rank + jnp.where((route_ref[0, s] == e) | (route_ref[1, s] == e), 1, 0)
            row.append(e * cap + rank)
        slots.append(row)

    x32, dy32 = x_ref[...].astype(f32), dy_ref[...].astype(f32)
    both8[0:tok, :] = x32
    both8[tok : 2 * tok, :] = dy32
    cot8[0:tok, :] = dy32
    cot8[tok : 2 * tok, :] = dy32

    def chosen_rows(offset):
        def test(row, col):
            hit = None
            for t in range(tok):
                mine = (row // segs == slots[t][0]) | (row // segs == slots[t][1])
                mine = mine & (col % (2 * tok) == offset + t)
                hit = mine if hit is None else hit | mine
            return hit & (row % segs == col // (2 * tok))

        return one_hot(lines, segs * 2 * tok, test)

    batches = [(0, start, size) for start, size in spans(X_CUTS, width)] + [(1, 0, width)]
    pick_rows = (chosen_rows(0), chosen_rows(tok))
    sends = []

    def pack(n):
        which, start, size = batches[n]
        step = size // segs
        stacked = jnp.concatenate(
            [both8[:, start + s * step : start + (s + 1) * step] for s in range(segs)], axis=0
        ).astype(bf16)
        lined = lax.dot_general(pick_rows[which], stacked, NN, preferred_element_type=f32)
        packs[n][...] = lined.astype(bf16).reshape(n_dp, TILE, step)

    def send(n):
        for k in range(1, n_dp):
            q = lax.rem(dp + k, n_dp)
            copy = remote(
                packs[n].at[q],
                recvs[n].at[grp, core, dp],
                in_sems.at[0, n, k],
                in_sems.at[1, n, k],
                place(grp, q, core),
            )
            copy.start()
            sends.append(copy)
        recvs[n][grp, core, dp] = packs[n][dp]

    pack(0)
    pl.semaphore_wait(barrier, n_dp + 1)
    send(0)
    pack(1)
    send(1)
    for copy in wide_loads[first_loads:]:
        copy.start()
    pack(2)

    def alone(body):
        pl.when(dp >= 0)(body)

    to_pair, to_far, pair_on = {}, {}, {}

    def pass_on(n):
        for k in range(1, n_dp):
            sends[n * (n_dp - 1) + k - 1].wait_recv()
        mine = recvs[n].at[grp, core]
        to_far[n] = remote(
            mine, mine, pass_sems.at[0, n], pass_sems.at[1, n], place(far, dp, core)
        )
        to_pair[n] = remote(
            mine, mine, pass_sems.at[2, n], pass_sems.at[3, n], place(grp, dp, other)
        )
        to_far[n].start()
        to_pair[n].start()

    def pass_far(n):
        to_far[n].wait_recv()
        theirs = recvs[n].at[far, core]
        pair_on[n] = remote(
            theirs, theirs, pass_sems.at[4, n], pass_sems.at[5, n], place(grp, dp, other)
        )
        pair_on[n].start()

    unmix = one_hot(
        lines, lines, lambda row, col: (row // quarter == col % segs) & (row % quarter == col // segs)
    )
    mix = one_hot(
        lines, lines, lambda row, col: (col // quarter == row % segs) & (col % quarter == row // segs)
    )

    def unpack(n, dest):
        which, start, size = batches[n]
        step = size // segs
        to_pair[n].wait_recv()
        pair_on[n].wait_recv()
        for g in range(2):
            for c in range(2):
                lined = recvs[n][g, c].reshape(lines, step)
                flat = lax.dot_general(unmix, lined, NN, preferred_element_type=f32).astype(bf16)
                top = (2 * g + c) * quarter
                for s in range(segs):
                    dest[top : top + quarter, start + s * step : start + (s + 1) * step] = flat[
                        s * quarter : (s + 1) * quarter, :
                    ]

    def multiply_in(n, between):
        _, start, size = batches[n]
        for m in range(start // ROWS_IN, (start + size) // ROWS_IN):
            wide_loads[2 * m].wait()
            wide_loads[2 * m + 1].wait()
        block = 2 * part // 4

        def some(first, end):
            for m in range(first, end):
                cols = slice(m * block, (m + 1) * block)
                term = lax.dot_general(
                    xs[:, start : start + size],
                    wide[start : start + size, cols],
                    NN,
                    preferred_element_type=f32,
                )
                pre[:, cols] = term if n == 0 else pre[:, cols] + term

        alone(lambda: some(0, 2))
        between()
        alone(lambda: some(2, 4))

    def first_between():
        pass_far(1)

    pass_on(0)
    send(2)
    for copy in down_loads:
        copy.start()
    pass_on(1)
    pass_far(0)
    unpack(0, xs)
    multiply_in(0, first_between)
    pass_on(2)
    unpack(1, xs)
    multiply_in(1, lambda: None)
    for copy in down_loads:
        copy.wait()

    def gate(m):
        block = part // 4
        cols = slice(m * block, (m + 1) * block)
        more = slice(part + m * block, part + (m + 1) * block)
        gate_pre, up_pre = pre[:, cols], pre[:, more]
        sig = 1.0 / (1.0 + jnp.exp(-gate_pre))
        return cols, more, gate_pre, up_pre, sig, gate_pre * sig

    def forward():
        for m in range(4):
            cols, _, _, up_pre, _, silu = gate(m)
            hid[:, cols] = (silu * up_pre).astype(bf16)

    def backward():
        for m in range(4):
            cols, more, gate_pre, up_pre, sig, silu = gate(m)
            d_hidden = lax.dot_general(down[cols, :], dys[...], NT, preferred_element_type=f32).T
            d_both[:, cols] = (d_hidden * up_pre * sig * (1.0 + gate_pre * (1.0 - sig))).astype(bf16)
            d_both[:, more] = (d_hidden * silu).astype(bf16)

    alone(forward)

    items = [(0, start, size) for start, size in spans(OUT_CUTS, width)]
    items += [(1, start, size) for start, size in spans(GRAD_CUTS, width)]
    pair_copies, side_copies, home_copies = {}, {}, {}

    def compute(i, between=None):
        which, start, size = items[i]
        cols = slice(start, start + size)

        def multiply(first=start):
            if which == 1:
                acc[1, :, cols] = lax.dot_general(
                    wide[cols, :], d_both[...], NT, preferred_element_type=f32
                ).T
                return
            block = min(size, 1024)
            for at in range(first, first + size // 2, block):
                acc[0, :, at : at + block] = lax.dot_general(
                    hid[...], down[:, at : at + block], NN, preferred_element_type=f32
                )

        alone(multiply)
        if which == 0:
            between()
            alone(lambda: multiply(start + size // 2))
        for g in range(2):
            give = pl.ds(pl.multiple_of((2 * g + other) * quarter, quarter), quarter)
            pair_send[which, g, :, cols] = acc[which, give, cols].astype(bf16)
        pair_copies[i] = remote(
            pair_send.at[which, :, :, pl.ds(start, size)],
            pair_recv.at[which, :, :, pl.ds(start, size)],
            ring_sems.at[0, i],
            ring_sems.at[1, i],
            place(grp, dp, other),
        )
        pair_copies[i].start()

    def to_side(i):
        which, start, size = items[i]
        cols = slice(start, start + size)
        pair_copies[i].wait_recv()

        def total(g):
            own = pl.ds(pl.multiple_of((2 * g + core) * quarter, quarter), quarter)
            return acc[which, own, cols] + pair_recv[which, g, :, cols].astype(f32)

        side_send[which, :, cols] = total(far).astype(bf16)
        side_copies[i] = remote(
            side_send.at[which, :, pl.ds(start, size)],
            side_recv.at[which, :, pl.ds(start, size)],
            ring_sems.at[2, i],
            ring_sems.at[3, i],
            place(far, dp, core),
        )
        side_copies[i].start()
        kept[which, :, cols] = total(grp)

    def to_home(i):
        which, start, size = items[i]
        step = size // segs
        side_copies[i].wait_recv()
        cols = slice(start, start + size)
        total = (kept[which, :, cols] + side_recv[which, :, cols].astype(f32)).astype(bf16)
        stacked = jnp.concatenate([total[:, s * step : (s + 1) * step] for s in range(segs)], axis=0)
        lined = lax.dot_general(mix, stacked, NN, preferred_element_type=f32).astype(bf16)
        back_sends[i][...] = lined.reshape(n_dp, TILE, step)
        home_copies[i] = []
        for k in range(1, n_dp):
            q = lax.rem(dp + k, n_dp)
            copy = remote(
                back_sends[i].at[q],
                back_recvs[i].at[dp],
                back_sems.at[0, i, k],
                back_sems.at[1, i, k],
                place(grp, q, core),
            )
            copy.start()
            home_copies[i].append(copy)
        back_recvs[i][dp] = back_sends[i][dp]

    def pick_test(row, col):
        hit = None
        for t in range(tok):
            for j in range(2):
                mine = (row % (2 * tok) == j * tok + t) & (col // segs == slots[t][j])
                hit = mine if hit is None else hit | mine
        return hit & (row // (2 * tok) == col % segs)

    pick = one_hot(segs * 2 * tok, lines, pick_test)
    share_rows = lax.broadcasted_iota(jnp.int32, (2 * tok, 1), 0)
    units = jnp.zeros((2 * tok, 1), jnp.int32)
    for t in range(tok):
        units = jnp.where(share_rows == t, first_ref[t], units)
        units = jnp.where(share_rows == tok + t, 1024 - first_ref[t], units)
    share = units.astype(f32) / 1024.0
    scores = []

    def finish(i):
        which, start, size = items[i]
        step = size // segs
        for copy in home_copies[i]:
            copy.wait_recv()
        got = lax.dot_general(
            pick, back_recvs[i][...].reshape(lines, step), NN, preferred_element_type=f32
        )
        for s in range(segs):
            cols = slice(start + s * step, start + (s + 1) * step)
            here = got[s * 2 * tok : (s + 1) * 2 * tok, :]
            weighted = here * share
            summed = (weighted[:tok] + weighted[tok:]).astype(bf16)
            if which == 0:
                mixed_ref[:, cols] = summed
                scores.append(jnp.sum(here * cot8[:, cols], axis=1, keepdims=True))
            else:
                grad_ref[:, cols] = summed

    compute(0, lambda: pass_far(2))
    unpack(2, dys)
    to_side(0)
    alone(backward)
    compute(1)
    to_home(0)
    compute(2)
    to_side(1)
    compute(3)
    to_side(2)
    to_home(1)
    compute(4)
    to_side(3)
    to_home(2)
    to_side(4)
    finish(0)
    to_home(3)
    finish(1)
    to_home(4)
    finish(2)
    finish(3)
    for copy in sends:
        copy.wait_send()
    for copies in (to_far, to_pair, pair_on, pair_copies, side_copies):
        for copy in copies.values():
            copy.wait_send()
    for copies in home_copies.values():
        for copy in copies:
            copy.wait_send()
    finish(4)

    score = scores[0]
    for more in scores[1:]:
        score = score + more
    row = lax.broadcasted_iota(jnp.int32, (2 * tok, tok), 0)
    col = lax.broadcasted_iota(jnp.int32, (2 * tok, tok), 1)
    for j in range(2):
        score_ref[j : j + 1, :] = jnp.sum(
            jnp.where(row == col + j * tok, score, 0.0), axis=0, keepdims=True
        )


def place_kernel(mixed_in, grad_in, score_in, mixed_out, grad_out, score_out):
    mixed_out[...] = mixed_in[...]
    grad_out[...] = grad_in[...]
    score_out[...] = score_in[...]


def fused(n_dp, tokens, cotangent, routing, gate_first, gate_weight, up_weight, down_weight):
    tok, width = tokens.shape
    cap = tok // 2
    segs = TILE // cap
    quarter = n_dp * cap
    rows = 4 * quarter
    hidden = down_weight.shape[0]
    part = hidden // 2
    f32, bf16 = jnp.float32, jnp.bfloat16
    vmem = pl.BlockSpec(memory_space=pltpu.VMEM)
    hbm = pl.BlockSpec(memory_space=pl.ANY)
    dma = pltpu.SemaphoreType.DMA
    steps_in = [size // segs for _, size in spans(X_CUTS, width)] + [width // segs]
    steps_out = [size // segs for _, size in spans(OUT_CUTS, width) + spans(GRAD_CUTS, width)]
    shapes = (
        jax.ShapeDtypeStruct((tok, width), bf16),
        jax.ShapeDtypeStruct((tok, width), bf16),
        jax.ShapeDtypeStruct((2, tok), f32),
    )
    results = pl.pallas_call(
        functools.partial(layer_kernel, n_dp),
        out_shape=shapes,
        in_specs=[hbm] * 7,
        out_specs=(vmem, vmem, vmem),
        scratch_shapes=[
            pltpu.SMEM((2, tok), jnp.int32),
            pltpu.SMEM((tok,), jnp.int32),
            pltpu.VMEM((tok, width), bf16),
            pltpu.VMEM((tok, width), bf16),
            pltpu.VMEM((width, 2 * part), bf16),
            pltpu.VMEM((part, width), bf16),
            pltpu.VMEM((2 * tok, width), f32),
            pltpu.VMEM((2 * tok, width), f32),
            pltpu.VMEM((rows, width), bf16),
            pltpu.VMEM((rows, width), bf16),
            pltpu.VMEM((rows, 2 * part), f32),
            pltpu.VMEM((rows, part), bf16),
            pltpu.VMEM((rows, 2 * part), bf16),
            pltpu.VMEM((2, rows, width), f32),
            pltpu.VMEM((2, 2, quarter, width), bf16),
            pltpu.VMEM((2, 2, quarter, width), bf16),
            pltpu.VMEM((2, quarter, width), f32),
            pltpu.VMEM((2, quarter, width), bf16),
            pltpu.VMEM((2, quarter, width), bf16),
            dma((4,)),
            dma((2 * (width // ROWS_IN) + part // ROWS_IN,)),
            dma((2, len(steps_in), n_dp)),
            dma((6, len(steps_in))),
            dma((4, len(steps_out))),
            dma((2, len(steps_out), n_dp)),
            [pltpu.VMEM((n_dp, TILE, step), bf16) for step in steps_in],
            [pltpu.VMEM((2, 2, n_dp, TILE, step), bf16) for step in steps_in],
            [pltpu.VMEM((n_dp, TILE, step), bf16) for step in steps_out],
            [pltpu.VMEM((n_dp, TILE, step), bf16) for step in steps_out],
        ],
        compiler_params=pltpu.CompilerParams(
            collective_id=0, has_side_effects=True, vmem_limit_bytes=61 * 1024 * 1024
        ),
    )(routing.T, gate_first, tokens, cotangent, gate_weight, up_weight, down_weight)
    mixed, grad, score = pl.pallas_call(
        place_kernel,
        out_shape=shapes,
        in_specs=[vmem] * 3,
        out_specs=(vmem, vmem, vmem),
    )(*results)
    return mixed, grad, score.T


def solution(mesh):
    placed = (
        P(("groups", "dp", "expert"), None),
        P(("groups", "dp", "expert"), None),
        P(("groups", "dp", "expert"), None),
        P(("groups", "dp", "expert")),
        P(None, ("dp", "expert")),
        P(None, ("dp", "expert")),
        P(("dp", "expert"), None),
    )
    n_dp = mesh.shape["dp"]
    two_groups = n_dp == E and mesh.shape["expert"] == 2 and mesh.shape["groups"] == 2
    return jax.shard_map(
        functools.partial(fused, n_dp) if two_groups else on_device,
        mesh=mesh,
        in_specs=placed,
        out_specs=(
            P(("groups", "dp", "expert"), None),
            P(("groups", "dp", "expert"), None),
            P(("groups", "dp", "expert"), None),
        ),
        check_vma=False,
    )
```
